32 devices in a mesh: panel: 4 (over y, core), tile: 4 (over z), lev: 2 (over x).
Axes of the slice: x: 2, y: 2, z: 4, core: 2. Of those that a mesh axis runs over, the one named last changes fastest.
Arguments:
- adjoint_new: float32 [5, 16, 32768], P(None, 'lev', ('panel', 'tile')), may hold values from -6 to 6
- weights: float32 [4, 32768], P(None, ('panel', 'tile', 'lev')), may hold values from 0.05 to 0.5
- departure: int32 [4, 32768], P(None, ('panel', 'tile')), may hold values from 0 to 2047
- send_point: int32 [4, 2048], P(None, ('panel', 'tile')), may hold values from 0 to 8191, as said below
- block_count: int32 [4, 16], P(None, ('panel', 'tile')), may hold values from 0 to 128, as said below
- rotation: int32 [2, 16], P(None, ('panel', 'tile')), may hold values from 0 to 3
Outputs:
- adjoint_old: float32 [5, 16, 32768], P(None, 'lev', ('panel', 'tile'))
The draws below stay inside these ranges and needn't reach their ends.
Inputs may be any that keep to these rules, and one draw needn't show every extreme that they name: `send_point`: within one tile the 512 entries are distinct stencil point numbers k * 2048 + c of that tile's own cells. `block_count`: zero for block 0 on the first tile and for block 1 on the last tile of each sector; every block position reaches 128 on some tile in every draw.
All inputs are finite; a program needn't handle non-finite values.
Results may differ from the reference program's by a relative error of at most 0.00002.
Values sent between devices are 32-bit elements; how exact they have to be, the bound alone decides.
No kernel may reach another device: no remote copies, remote signals or barrier semaphores. Data moves between devices by JAX's collectives and lax.ppermute only.
A program may use at most 64 MiB of HBM per device.

```python
import jax
import jax.numpy as jnp
from jax import lax

FIELDS = 5
STENCIL = 4
SLOTS = 128
CELLS_DEV = 2048
CELLS = 32768
LEVELS = 16
N_PANEL = 4
N_TILE = 4


def draw_send_point(key, part):
    devices = N_PANEL * N_TILE
    keys = jax.random.split(jax.random.fold_in(key, 11), devices)

    def one_tile(tile_key):
        order = jax.random.permutation(tile_key, STENCIL * CELLS_DEV)
        return order[:4 * SLOTS].reshape(4, SLOTS)
    picks = jax.vmap(one_tile)(keys)
    return jnp.transpose(picks, (1, 0, 2)).reshape(4, devices * SLOTS).astype(jnp.int32)


def draw_block_count(key, part):
    devices = N_PANEL * N_TILE
    base_key = jax.random.fold_in(key, 23)
    key_low, key_high, key_busy, key_panel, key_tile = jax.random.split(base_key, 5)
    low_count = jax.random.randint(key_low, (4, devices), SLOTS // 8, SLOTS // 2 + 1)
    high_count = jax.random.randint(key_high, (4, devices), 3 * SLOTS // 4, SLOTS + 1)
    busy_tile = jax.random.randint(key_busy, (4, devices), 0, 8) == 0
    counts = jnp.where(busy_tile, high_count, low_count)
    device = jnp.arange(devices, dtype=jnp.int32)
    panel_of = device // N_TILE
    tile_of = device % N_TILE
    pick_panel = jax.random.randint(key_panel, (4,), 0, N_PANEL)
    pick_tile = jax.random.randint(key_tile, (4,), 1, N_TILE - 1)
    full_tile = (panel_of[None, :] == pick_panel[:, None]) & (tile_of[None, :] == pick_tile[:, None])
    counts = jnp.where(full_tile, SLOTS, counts)
    edge_zero = jnp.stack([tile_of == 0, tile_of == N_TILE - 1, tile_of < 0, tile_of < 0])
    counts = jnp.where(edge_zero, 0, counts)
    return counts.astype(jnp.int32)


def touch_ends(drawn, stream_key, low, largest):
    dims = drawn.shape
    place = [jax.random.randint(jax.random.fold_in(stream_key, axis), (), 0, dims[axis]) for axis in range(len(dims))]
    drawn = drawn.at[tuple(place)].set(low)
    longest = dims.index(max(dims))
    place[longest] = (place[longest] + 1) % dims[longest]
    return drawn.at[tuple(place)].set(largest)


def block_levels(own_key, extent, shards, least, largest):
    loudness = 1.0
    for dim, parts in shards:
        steps = jax.random.uniform(jax.random.fold_in(jax.random.fold_in(own_key, 6), dim), (parts,), jnp.float32, least / len(shards), largest / len(shards))
        loudness = loudness * jnp.repeat(jnp.exp(steps), extent[dim] // parts).reshape((-1,) + (1,) * (len(extent) - 1 - dim))
    return loudness


def scatter_about(key, dims, deviation, bound, pieces=(), kind=jnp.bfloat16):
    result = jax.random.normal(key, dims, jnp.float32) * deviation
    if len(pieces) > 0:
        result = block_levels(key, dims, pieces, -0.22, 0.18) * result
    return jnp.clip(result, min=-bound, max=bound).astype(kind)


def setup_inputs(seed: int = 0) -> dict:
    streams_of = jax.random.split(jax.random.key(seed), 7)
    return {
        "adjoint_new": scatter_about(streams_of[0], (FIELDS, LEVELS, CELLS), 1.0, 6.0, ((1, 2), (2, 16)), jnp.float32),
        "weights": jnp.clip(0.05 + 0.45 * jax.random.uniform(streams_of[1], (STENCIL, CELLS), jnp.float32) ** block_levels(streams_of[1], (STENCIL, CELLS), ((1, 32),), -0.2, 0.2), 0.05, 0.5),
        "departure": touch_ends(jax.random.randint(streams_of[2], (STENCIL, CELLS), 0, CELLS_DEV), jax.random.fold_in(streams_of[2], 1), 0, CELLS_DEV - 1).astype(jnp.int32),
        "send_point": draw_send_point(jax.random.fold_in(streams_of[6], 71), 0),
        "block_count": draw_block_count(jax.random.fold_in(streams_of[6], 71), 0),
        "rotation": touch_ends(jax.random.randint(streams_of[5], (2, N_PANEL * N_TILE), 0, 4), jax.random.fold_in(streams_of[5], 1), 0, 3).astype(jnp.int32),
    }


def routing(departure, send_point, block_count, rotation):
    devices = N_PANEL * N_TILE
    points = STENCIL * CELLS
    column = jnp.arange(CELLS, dtype=jnp.int32)
    home_base = (column // CELLS_DEV) * CELLS_DEV
    target = (home_base[None, :] + departure).reshape(-1)
    device = jnp.arange(devices, dtype=jnp.int32)
    panel_of = device // N_TILE
    tile_of = device % N_TILE
    owners = jnp.stack([panel_of * N_TILE + tile_of - 1, panel_of * N_TILE + tile_of + 1, ((panel_of + N_PANEL - 1) % N_PANEL) * N_TILE + tile_of, ((panel_of + 1) % N_PANEL) * N_TILE + tile_of])
    chosen = send_point.reshape(4, devices, SLOTS)
    stencil_row = chosen // CELLS_DEV
    cell_col = device[None, :, None] * CELLS_DEV + chosen % CELLS_DEV
    landing = departure[stencil_row, cell_col]
    sent_target = owners[:, :, None] * CELLS_DEV + landing
    live_mask = jnp.arange(SLOTS, dtype=jnp.int32)[None, None, :] < block_count[:, :, None]
    flat_slot = jnp.where(live_mask, stencil_row * CELLS + cell_col, points).reshape(-1)
    target = target.at[flat_slot].set(sent_target.reshape(-1), mode="drop")
    turn_rows = jnp.concatenate([jnp.zeros((2, devices), jnp.int32), rotation], axis=0)
    spread_turn = jnp.broadcast_to(turn_rows[:, :, None], (4, devices, SLOTS)).reshape(-1)
    turn_code = jnp.zeros((points,), jnp.int32).at[flat_slot].set(spread_turn, mode="drop")
    return target.reshape(STENCIL, CELLS), turn_code.reshape(STENCIL, CELLS)


def reference(adjoint_new, weights, departure, send_point, block_count, rotation):
    target, turn_code = routing(departure, send_point, block_count, rotation)
    by_cell = jnp.transpose(adjoint_new, (2, 0, 1))
    cosine = (turn_code == 0).astype(jnp.float32) - (turn_code == 2).astype(jnp.float32)
    sine_term = (turn_code == 1).astype(jnp.float32) - (turn_code == 3).astype(jnp.float32)

    def one_point(summed, point_k):
        cosine_k = cosine[point_k][:, None]
        sine_k = sine_term[point_k][:, None]
        zonal_part = by_cell[:, 0, :]
        merid_part = by_cell[:, 1, :]
        turned = jnp.concatenate([(cosine_k * zonal_part + sine_k * merid_part)[:, None, :], (cosine_k * merid_part - sine_k * zonal_part)[:, None, :], by_cell[:, 2:, :]], axis=1)
        turned = turned * weights[point_k][:, None, None]
        return summed.at[target[point_k]].add(turned), None

    summed, _ = lax.scan(one_point, jnp.zeros(by_cell.shape, adjoint_new.dtype), jnp.arange(STENCIL, dtype=jnp.int32))
    return jnp.transpose(summed, (1, 2, 0))
```

```python
import jax
import jax.numpy as jnp
from jax import lax
from jax.experimental import pallas as pl
from jax.experimental.pallas import tpu as pltpu
from jax.sharding import PartitionSpec as P

F32, BF16, I32 = jnp.float32, jnp.bfloat16, jnp.int32
LO = 256
LANES = 128
SUB = 8
VMEM = pl.BlockSpec(memory_space=pltpu.VMEM)
SMEM = pl.BlockSpec(memory_space=pltpu.SMEM)
PARAMS = pltpu.CompilerParams(vmem_limit_bytes=32 << 20)


def two_terms(value):
    high = value.astype(BF16).astype(F32)
    return jnp.concatenate([high, value - high], axis=0)


def place_weights(parts, full):
    count = len(parts)
    width = parts[0].shape[1]
    me = lax.axis_index("lev")
    for s, part in enumerate(parts):
        source = lax.rem(me + (count - s), count)
        full[:, pl.ds(pl.multiple_of(source * width, LANES), width)] = part[...]


def scatter_product(terms, target, cells):
    points = target.shape[1]
    high = target // LO
    low = target - high * LO
    left = jnp.concatenate(
        [terms * (high == h).astype(F32).astype(BF16) for h in range(cells // LO)], axis=0
    )
    lane = lax.broadcasted_iota(I32, (LO, points), 0)
    right = (lane == low).astype(F32).astype(BF16)
    return lax.dot_general(
        left, right, (((1,), (1,)), ((), ())), preferred_element_type=F32
    )


def pick_kernel(count, levels, u_ref, dep_ref, sp_ref, bc_ref, rot_ref, *refs):
    parts, outs, full = refs[:count], refs[count:-1], refs[-1]
    rows, cells = u_ref.shape
    stencil = dep_ref.shape[0]
    blocks, slots = sp_ref.shape
    place_weights(parts, full)
    dep = dep_ref[...]
    dep_high = dep // SUB
    dep_low = dep - dep_high * SUB
    w = full[...]
    w0 = w.astype(BF16).astype(F32)
    w1 = (w - w0).astype(BF16).astype(F32)
    table = jnp.concatenate(
        [
            two_terms(u_ref[...]),
            jnp.concatenate([dep_high.astype(F32), dep_low.astype(F32)], axis=0),
            jnp.concatenate([w0, w1], axis=0),
            jnp.concatenate([w - w0 - w1, jnp.zeros_like(w)], axis=0),
            jnp.zeros((SUB, cells), F32),
        ],
        axis=0,
    ).astype(BF16)
    chosen = [sp_ref[j : j + 1, :] for j in range(blocks)]
    which = [c // cells for c in chosen]
    column = jnp.concatenate([c - k * cells for c, k in zip(chosen, which)], axis=1)
    cell = lax.broadcasted_iota(I32, (cells, blocks * slots), 0)
    onehot = (cell == column).astype(F32).astype(BF16)
    got = jnp.dot(table, onehot, preferred_element_type=F32)
    slot = lax.broadcasted_iota(I32, (1, slots), 1)
    d0 = 2 * rows
    w0 = d0 + 2 * stencil
    for j in range(blocks):
        g = got[:, j * slots : (j + 1) * slots]
        ids = jnp.zeros((1, slots), F32)
        weight = jnp.zeros((1, slots), F32)
        for k in range(stencil):
            hit = which[j] == k
            one_id = g[d0 + k : d0 + k + 1] * SUB + g[d0 + stencil + k : d0 + stencil + k + 1]
            one_w = (
                g[w0 + k : w0 + k + 1]
                + g[w0 + stencil + k : w0 + stencil + k + 1]
                + g[w0 + 2 * stencil + k : w0 + 2 * stencil + k + 1]
            )
            ids = ids + jnp.where(hit, one_id, 0.0)
            weight = weight + jnp.where(hit, one_w, 0.0)
        weight = jnp.where(slot < bc_ref[j], weight, 0.0)
        values = (g[:rows] + g[rows : 2 * rows]) * weight
        zonal, merid = values[:levels], values[levels : 2 * levels]
        if j >= 2:
            code = rot_ref[j - 2]
            cosine = (code == 0).astype(F32) - (code == 2).astype(F32)
            sine = (code == 1).astype(F32) - (code == 3).astype(F32)
            zonal, merid = cosine * zonal + sine * merid, cosine * merid - sine * zonal
        out = outs[j]
        out[:levels, :] = zonal
        out[levels : 2 * levels, :] = merid
        out[2 * levels : rows, :] = values[2 * levels :]
        out[rows:, :] = jnp.broadcast_to(ids, (SUB, slots))


def local_kernel(count, u_ref, dep_ref, sp_ref, bc_ref, *refs):
    parts, out_ref, full, acc = refs[:count], refs[-3], refs[-2], refs[-1]
    rows, cells = u_ref.shape
    stencil = dep_ref.shape[0]
    blocks, slots = sp_ref.shape
    tiles = cells // LANES
    place_weights(parts, full)
    slot = lax.broadcasted_iota(I32, (1, slots), 1)
    codes, lanes = [], []
    for j in range(blocks):
        chosen = sp_ref[j : j + 1, :]
        which = chosen // cells
        column = chosen - which * cells
        tile = column // LANES
        codes.append(jnp.where(slot < bc_ref[j], tile * SUB + which, -1))
        lanes.append(column - tile * LANES)
    shape = (tiles * SUB, blocks * slots)
    row = lax.broadcasted_iota(I32, shape, 0)
    left = (row == jnp.concatenate(codes, axis=1)).astype(F32).astype(BF16)
    lane_row = lax.broadcasted_iota(I32, (LANES, blocks * slots), 0)
    right = (lane_row == jnp.concatenate(lanes, axis=1)).astype(F32).astype(BF16)
    sent = lax.dot_general(
        left, right, (((1,), (1,)), ((), ())), preferred_element_type=F32
    )
    for t in range(tiles):
        at = slice(t * LANES, (t + 1) * LANES)
        full[:, at] = full[:, at] * (1.0 - sent[t * SUB : t * SUB + stencil])
    acc[...] = jnp.zeros_like(acc)

    def one_point(k, _):
        value = u_ref[...] * full[pl.ds(k, 1), :]
        terms = two_terms(value).astype(BF16)
        acc[...] += scatter_product(terms, dep_ref[pl.ds(k, 1), :], cells)
        return 0

    lax.fori_loop(0, stencil, one_point, 0)
    for h in range(cells // LO):
        at = h * 2 * rows
        out_ref[:, h * LO : (h + 1) * LO] = acc[at : at + rows] + acc[at + rows : at + 2 * rows]


def arrive_kernel(local_ref, *refs):
    received, out_ref = refs[:-1], refs[-1]
    rows, cells = local_ref.shape
    values = jnp.concatenate([r[:rows, :] for r in received], axis=1)
    ids = jnp.concatenate([r[rows : rows + 1, :] for r in received], axis=1).astype(I32)
    sums = scatter_product(two_terms(values).astype(BF16), ids, cells)
    for h in range(cells // LO):
        at = h * 2 * rows
        span = slice(h * LO, (h + 1) * LO)
        out_ref[:, span] = local_ref[:, span] + (sums[at : at + rows] + sums[at + rows : at + 2 * rows])


def shifted(value, axis, distance):
    devices = range(lax.axis_size(axis))
    return lax.ppermute(value, axis, [(i - distance, i) for i in devices if i - distance in devices])


def rotated(value, axis, steps):
    count = lax.axis_size(axis)
    return lax.ppermute(value, axis, [(i, (i + steps) % count) for i in range(count)])


def body(adjoint_new, weights, departure, send_point, block_count, rotation):
    fields, levels, cells = adjoint_new.shape
    blocks, slots = send_point.shape
    stencil = departure.shape[0]
    rows = fields * levels
    count = lax.axis_size("lev")
    u = adjoint_new.reshape(rows, cells)
    bc = block_count.reshape(-1)
    rot = rotation.reshape(-1)
    parts = [weights] + [rotated(weights, "lev", s) for s in range(1, count)]
    full = pltpu.VMEM((stencil, cells), F32)
    block = jax.ShapeDtypeStruct((rows + SUB, slots), F32)
    outgoing = pl.pallas_call(
        lambda *refs: pick_kernel(count, levels, *refs),
        out_shape=[block] * blocks,
        in_specs=[VMEM, VMEM, VMEM, SMEM, SMEM] + [VMEM] * count,
        out_specs=[VMEM] * blocks,
        scratch_shapes=[full],
        cost_estimate=pl.CostEstimate(
            flops=4 * rows * cells * blocks * slots, bytes_accessed=4 * rows * cells, transcendentals=0
        ),
        compiler_params=PARAMS,
        name="pick",
    )(u, departure, send_point, bc, rot, *parts)
    received = [
        shifted(outgoing[1], "tile", 1),
        shifted(outgoing[0], "tile", -1),
        rotated(outgoing[3], "panel", 1),
        rotated(outgoing[2], "panel", -1),
    ]
    result = jax.ShapeDtypeStruct((rows, cells), F32)
    local = pl.pallas_call(
        lambda *refs: local_kernel(count, *refs),
        out_shape=result,
        in_specs=[VMEM, VMEM, VMEM, SMEM] + [VMEM] * count,
        out_specs=VMEM,
        scratch_shapes=[full, pltpu.VMEM((cells // LO * 2 * rows, LO), F32)],
        cost_estimate=pl.CostEstimate(
            flops=4 * rows * cells * stencil * cells, bytes_accessed=8 * rows * cells, transcendentals=0
        ),
        compiler_params=PARAMS,
        name="local",
    )(u, departure, send_point, bc, *parts)
    out = pl.pallas_call(
        arrive_kernel,
        out_shape=result,
        in_specs=[VMEM] * (1 + blocks),
        out_specs=VMEM,
        compiler_params=PARAMS,
        name="arrive",
    )(local, *received)
    return out.reshape(fields, levels, cells)


def solution(mesh):
    return jax.shard_map(
        body,
        mesh=mesh,
        in_specs=(
            P(None, "lev", ("panel", "tile")),
            P(None, ("panel", "tile", "lev")),
            P(None, ("panel", "tile")),
            P(None, ("panel", "tile")),
            P(None, ("panel", "tile")),
            P(None, ("panel", "tile")),
        ),
        out_specs=P(None, "lev", ("panel", "tile")),
        check_vma=False,
    )
```

```python
import jax
import jax.numpy as jnp
from jax import lax
from jax.experimental import pallas as pl
from jax.experimental.pallas import tpu as pltpu
from jax.sharding import PartitionSpec as P

F32, BF16, I32 = jnp.float32, jnp.bfloat16, jnp.int32
LO = 256
LANES = 128
SUB = 8
VMEM = pl.BlockSpec(memory_space=pltpu.VMEM)
HBM = pl.BlockSpec(memory_space=pltpu.HBM)
PARAMS = pltpu.CompilerParams(vmem_limit_bytes=32 << 20)
NT = (((1,), (1,)), ((), ()))


def one_hot(rows, index):
    row = lax.broadcasted_iota(I32, (rows, index.shape[1]), 0)
    return (row == index).astype(F32).astype(BF16)


def two_terms(value):
    high = value.astype(BF16).astype(F32)
    return jnp.concatenate([high, value - high], axis=0)


def scatter_product(terms, target, cells):
    high = target // LO
    low = target - high * LO
    left = jnp.concatenate(
        [terms * (high == h).astype(F32).astype(BF16) for h in range(cells // LO)], axis=0
    )
    return lax.dot_general(left, one_hot(LO, low), NT, preferred_element_type=F32)


def prepare_kernel(
    levels, u_hbm, w_hbm, dep_hbm, sp_hbm, bc_hbm, rot_hbm,
    u_ref, w_ref, dep_ref, keep_ref, picked_ref, live_ref, lane_ref,
    sp_ref, bc_ref, rot_ref, sems,
):
    pairs = [(sp_hbm, sp_ref), (bc_hbm, bc_ref), (rot_hbm, rot_ref), (dep_hbm, dep_ref), (u_hbm, u_ref), (w_hbm, w_ref)]
    copies = [pltpu.make_async_copy(a, b, sems.at[i]) for i, (a, b) in enumerate(pairs)]
    for c in copies:
        c.start()
    for c in copies[:3]:
        c.wait()
    rows, cells = u_ref.shape
    stencil = dep_ref.shape[0]
    blocks, slots = sp_ref.shape
    tiles = cells // LANES
    slot = lax.broadcasted_iota(I32, (1, slots), 1)
    which, columns, codes, lanes = [], [], [], []
    for j in range(blocks):
        chosen = sp_ref[j : j + 1, :]
        k = chosen // cells
        column = chosen - k * cells
        tile = column // LANES
        which.append(k)
        columns.append(column)
        codes.append(jnp.where(slot < bc_ref[0:1, j : j + 1], tile * SUB + k, -1))
        lanes.append(column - tile * LANES)
    live = one_hot(tiles * SUB, jnp.concatenate(codes, axis=1))
    lane = one_hot(LANES, jnp.concatenate(lanes, axis=1))
    live_ref[...] = live
    lane_ref[...] = lane
    sent = lax.dot_general(live, lane, NT, preferred_element_type=F32)
    for t in range(tiles):
        keep_ref[:, t * LANES : (t + 1) * LANES] = 1.0 - sent[t * SUB : t * SUB + stencil]
    onehot = one_hot(cells, jnp.concatenate(columns, axis=1))
    for c in copies[3:]:
        c.wait()
    dep = dep_ref[...]
    dep_high = dep // SUB
    dep_low = dep - dep_high * SUB
    table = jnp.concatenate(
        [two_terms(u_ref[...]), jnp.concatenate([dep_high.astype(F32), dep_low.astype(F32)], axis=0), jnp.zeros((SUB, cells), F32)],
        axis=0,
    ).astype(BF16)
    got = jnp.dot(table, onehot, preferred_element_type=F32)
    at = 2 * rows
    for j in range(blocks):
        here = slice(j * slots, (j + 1) * slots)
        g = got[:, here]
        ids = jnp.zeros((1, slots), F32)
        for k in range(stencil):
            one_id = g[at + k : at + k + 1] * SUB + g[at + stencil + k : at + stencil + k + 1]
            ids = ids + jnp.where(which[j] == k, one_id, 0.0)
        values = g[:rows] + g[rows : 2 * rows]
        zonal, merid = values[:levels], values[levels : 2 * levels]
        if j >= 2:
            code = rot_ref[0:1, j - 2 : j - 1]
            cosine = (code == 0).astype(F32) - (code == 2).astype(F32)
            sine = (code == 1).astype(F32) - (code == 3).astype(F32)
            zonal, merid = cosine * zonal + sine * merid, cosine * merid - sine * zonal
        picked_ref[:levels, here] = zonal
        picked_ref[levels : 2 * levels, here] = merid
        picked_ref[2 * levels : rows, here] = values[2 * levels :]
        picked_ref[rows:, here] = jnp.broadcast_to(ids, (SUB, slots))


def place_weights(parts, full):
    count = len(parts)
    width = parts[0].shape[1]
    me = lax.axis_index("lev")
    for s, part in enumerate(parts):
        source = lax.rem(me + (count - s), count)
        full[:, pl.ds(pl.multiple_of(source * width, LANES), width)] = part[...]


def send_kernel(count, paired, picked_ref, live_ref, lane_ref, keep_ref, *refs):
    parts, outs, masked_ref, full = refs[:count], refs[count:-2], refs[-2], refs[-1]
    stencil, cells = full.shape
    rows = picked_ref.shape[0] - SUB
    blocks, slots = len(outs), outs[0].shape[1]
    place_weights(parts, full)
    pad = jnp.zeros((SUB - stencil, LANES), F32)
    pieces = []
    for t in range(cells // LANES):
        pieces += [full[:, t * LANES : (t + 1) * LANES], pad]
    w = jnp.concatenate(pieces, axis=0)
    w0 = w.astype(BF16).astype(F32)
    w1 = (w - w0).astype(BF16).astype(F32)
    terms = jnp.concatenate([w0, w1, w - w0 - w1], axis=0).astype(BF16)
    got = jnp.dot(terms, lane_ref[...], preferred_element_type=F32)
    n = w.shape[0]
    got = (got[:n] + got[n : 2 * n] + got[2 * n :]) * live_ref[...].astype(F32)
    weight = jnp.sum(got, axis=0, keepdims=True)
    message = [
        jnp.concatenate(
            [picked_ref[:rows, j * slots : (j + 1) * slots] * weight[:, j * slots : (j + 1) * slots], picked_ref[rows:, j * slots : (j + 1) * slots]],
            axis=0,
        )
        for j in range(blocks)
    ]
    if paired:
        even = lax.rem(lax.axis_index("panel"), 2) == 0
        low, high, previous, following = message
        message = [
            jnp.where(even, high, low),
            jnp.where(even, low, high),
            jnp.where(even, following, previous),
            jnp.where(even, previous, following),
        ]
    for out, m in zip(outs, message):
        out[...] = m
    masked_ref[...] = full[...] * keep_ref[...]


def local_kernel(u_ref, dep_ref, w_ref, out_ref, acc):
    rows, cells = u_ref.shape
    stencil = dep_ref.shape[0]
    acc[...] = jnp.zeros_like(acc)

    def one_point(k, _):
        value = u_ref[...] * w_ref[pl.ds(k, 1), :]
        terms = two_terms(value).astype(BF16)
        acc[...] += scatter_product(terms, dep_ref[pl.ds(k, 1), :], cells)
        return 0

    lax.fori_loop(0, stencil, one_point, 0)
    for h in range(cells // LO):
        at = h * 2 * rows
        out_ref[:, h * LO : (h + 1) * LO] = acc[at : at + rows] + acc[at + rows : at + 2 * rows]


def arrive_kernel(local_ref, *refs):
    received, out_ref = refs[:-1], refs[-1]
    rows, cells = local_ref.shape
    values = jnp.concatenate([r[:rows, :] for r in received], axis=1)
    ids = jnp.concatenate([r[rows : rows + 1, :] for r in received], axis=1).astype(I32)
    sums = scatter_product(two_terms(values).astype(BF16), ids, cells)
    for h in range(cells // LO):
        at = h * 2 * rows
        span = slice(h * LO, (h + 1) * LO)
        out_ref[:, span] = local_ref[:, span] + (sums[at : at + rows] + sums[at + rows : at + 2 * rows])


def rotated(value, axis, steps):
    count = lax.axis_size(axis)
    return lax.ppermute(value, axis, [(i, (i + steps) % count) for i in range(count)])


def racetrack(value, reverse):
    sectors, tiles = lax.axis_size("panel"), lax.axis_size("tile")
    route = []
    for p in range(sectors):
        step = 1 if (p % 2 == 0) != reverse else -1
        for t in range(tiles):
            q, to = (p, t + step) if 0 <= t + step < tiles else (p ^ 1, t)
            route.append((p * tiles + t, q * tiles + to))
    return lax.ppermute(value, ("panel", "tile"), route)


def swapped(value, outer):
    count = lax.axis_size("panel")
    step = [1, -1] if not outer else [-1, 1]
    return lax.ppermute(value, "panel", [(i, (i + step[i % 2]) % count) for i in range(count)])


def body(adjoint_new, weights, departure, send_point, block_count, rotation):
    fields, levels, cells = adjoint_new.shape
    blocks, slots = send_point.shape
    stencil = departure.shape[0]
    rows = fields * levels
    count = lax.axis_size("lev")
    paired = lax.axis_size("panel") % 2 == 0
    points = blocks * slots
    shape = jax.ShapeDtypeStruct
    parts = [rotated(weights, "lev", s) for s in range(1, count)]
    inputs = (
        adjoint_new.reshape(rows, cells), weights, departure, send_point,
        block_count.reshape(1, -1), rotation.reshape(1, -1),
    )
    u, own, dep, keep, picked, live, lane = pl.pallas_call(
        lambda *refs: prepare_kernel(levels, *refs),
        out_shape=[
            shape((rows, cells), F32),
            shape(weights.shape, F32),
            shape((stencil, cells), I32),
            shape((stencil, cells), F32),
            shape((rows + SUB, points), F32),
            shape((cells // LANES * SUB, points), BF16),
            shape((LANES, points), BF16),
        ],
        in_specs=[HBM] * 6,
        out_specs=[VMEM] * 7,
        scratch_shapes=[
            pltpu.VMEM((blocks, slots), I32),
            pltpu.VMEM((1, block_count.size), I32),
            pltpu.VMEM((1, rotation.size), I32),
            pltpu.SemaphoreType.DMA((6,)),
        ],
        cost_estimate=pl.CostEstimate(
            flops=4 * rows * cells * points, bytes_accessed=8 * rows * cells, transcendentals=0
        ),
        compiler_params=PARAMS,
        name="prepare",
    )(*(pltpu.with_memory_space_constraint(a, pltpu.HBM) for a in inputs))
    block = shape((rows + SUB, slots), F32)
    *outgoing, masked = pl.pallas_call(
        lambda *refs: send_kernel(count, paired, *refs),
        out_shape=[block] * blocks + [shape((stencil, cells), F32)],
        in_specs=[VMEM] * (4 + count),
        out_specs=[VMEM] * (blocks + 1),
        scratch_shapes=[pltpu.VMEM((stencil, cells), F32)],
        compiler_params=PARAMS,
        name="send",
    )(picked, live, lane, keep, own, *parts)
    if paired:
        received = [
            racetrack(outgoing[0], False),
            racetrack(outgoing[1], True),
            swapped(outgoing[2], False),
            swapped(outgoing[3], True),
        ]
    else:
        received = [
            rotated(outgoing[1], "tile", 1),
            rotated(outgoing[0], "tile", -1),
            rotated(outgoing[3], "panel", 1),
            rotated(outgoing[2], "panel", -1),
        ]
    result = shape((rows, cells), F32)
    local = pl.pallas_call(
        local_kernel,
        out_shape=result,
        in_specs=[VMEM] * 3,
        out_specs=VMEM,
        scratch_shapes=[pltpu.VMEM((cells // LO * 2 * rows, LO), F32)],
        cost_estimate=pl.CostEstimate(
            flops=4 * rows * cells * stencil * cells, bytes_accessed=8 * rows * cells, transcendentals=0
        ),
        compiler_params=PARAMS,
        name="local",
    )(u, dep, masked)
    out = pl.pallas_call(
        arrive_kernel,
        out_shape=result,
        in_specs=[VMEM] * (1 + blocks),
        out_specs=VMEM,
        compiler_params=PARAMS,
        name="arrive",
    )(local, *received)
    return out.reshape(fields, levels, cells)


def solution(mesh):
    return jax.shard_map(
        body,
        mesh=mesh,
        in_specs=(
            P(None, "lev", ("panel", "tile")),
            P(None, ("panel", "tile", "lev")),
            P(None, ("panel", "tile")),
            P(None, ("panel", "tile")),
            P(None, ("panel", "tile")),
            P(None, ("panel", "tile")),
        ),
        out_specs=P(None, "lev", ("panel", "tile")),
        check_vma=False,
    )
```

```python
import jax
import jax.numpy as jnp
from jax import lax
from jax.experimental import pallas as pl
from jax.experimental.pallas import tpu as pltpu
from jax.sharding import PartitionSpec as P

F32, BF16, I32 = jnp.float32, jnp.bfloat16, jnp.int32
LO = 256
LANES = 128
SUB = 8
VMEM = pl.BlockSpec(memory_space=pltpu.VMEM)
HBM = pl.BlockSpec(memory_space=pltpu.HBM)
PARAMS = pltpu.CompilerParams(vmem_limit_bytes=32 << 20)
NT = (((1,), (1,)), ((), ()))


def one_hot(rows, index):
    row = lax.broadcasted_iota(I32, (rows, index.shape[1]), 0)
    return (row == index).astype(F32).astype(BF16)


def two_terms(value):
    high = value.astype(BF16).astype(F32)
    return jnp.concatenate([high, value - high], axis=0)


def scatter_product(segments, cells):
    left = [[] for _ in range(cells // LO)]
    right = []
    for terms, target in segments:
        high = target // LO
        for h, row in enumerate(left):
            row.append(terms * (high == h).astype(F32).astype(BF16))
        right.append(one_hot(LO, target - high * LO))
    left = jnp.concatenate([jnp.concatenate(row, axis=1) for row in left], axis=0)
    return lax.dot_general(left, jnp.concatenate(right, axis=1), NT, preferred_element_type=F32)


def prepare_kernel(
    levels, u_hbm, w_hbm, dep_hbm, sp_hbm, bc_hbm, rot_hbm,
    u_ref, w_ref, dep_ref, keep_ref, picked_ref, live_ref, lane_ref,
    sp_ref, bc_ref, rot_ref, sems,
):
    pairs = [(sp_hbm, sp_ref), (bc_hbm, bc_ref), (rot_hbm, rot_ref), (dep_hbm, dep_ref), (u_hbm, u_ref), (w_hbm, w_ref)]
    copies = [pltpu.make_async_copy(a, b, sems.at[i]) for i, (a, b) in enumerate(pairs)]
    for c in copies:
        c.start()
    for c in copies[:3]:
        c.wait()
    rows, cells = u_ref.shape
    stencil = dep_ref.shape[0]
    blocks, slots = sp_ref.shape
    tiles = cells // LANES
    slot = lax.broadcasted_iota(I32, (1, slots), 1)
    which, columns, codes, lanes = [], [], [], []
    for j in range(blocks):
        chosen = sp_ref[j : j + 1, :]
        k = chosen // cells
        column = chosen - k * cells
        tile = column // LANES
        which.append(k)
        columns.append(column)
        codes.append(jnp.where(slot < bc_ref[0:1, j : j + 1], tile * SUB + k, -1))
        lanes.append(column - tile * LANES)
    live = one_hot(tiles * SUB, jnp.concatenate(codes, axis=1))
    lane = one_hot(LANES, jnp.concatenate(lanes, axis=1))
    live_ref[...] = live
    lane_ref[...] = lane
    sent = lax.dot_general(live, lane, NT, preferred_element_type=F32)
    for t in range(tiles):
        keep_ref[:, t * LANES : (t + 1) * LANES] = 1.0 - sent[t * SUB : t * SUB + stencil]
    onehot = one_hot(cells, jnp.concatenate(columns, axis=1))
    for c in copies[3:]:
        c.wait()
    dep = dep_ref[...]
    dep_high = dep // SUB
    dep_low = dep - dep_high * SUB
    table = jnp.concatenate(
        [two_terms(u_ref[...]), jnp.concatenate([dep_high.astype(F32), dep_low.astype(F32)], axis=0), jnp.zeros((SUB, cells), F32)],
        axis=0,
    ).astype(BF16)
    got = jnp.dot(table, onehot, preferred_element_type=F32)
    at = 2 * rows
    for j in range(blocks):
        here = slice(j * slots, (j + 1) * slots)
        g = got[:, here]
        ids = jnp.zeros((1, slots), F32)
        for k in range(stencil):
            one_id = g[at + k : at + k + 1] * SUB + g[at + stencil + k : at + stencil + k + 1]
            ids = ids + jnp.where(which[j] == k, one_id, 0.0)
        values = g[:rows] + g[rows : 2 * rows]
        zonal, merid = values[:levels], values[levels : 2 * levels]
        if j >= 2:
            code = rot_ref[0:1, j - 2 : j - 1]
            cosine = (code == 0).astype(F32) - (code == 2).astype(F32)
            sine = (code == 1).astype(F32) - (code == 3).astype(F32)
            zonal, merid = cosine * zonal + sine * merid, cosine * merid - sine * zonal
        picked_ref[:levels, here] = zonal
        picked_ref[levels : 2 * levels, here] = merid
        picked_ref[2 * levels : rows, here] = values[2 * levels :]
        picked_ref[rows:, here] = jnp.broadcast_to(ids, (SUB, slots))


def place_weights(parts, full):
    count = len(parts)
    width = parts[0].shape[1]
    me = lax.axis_index("lev")
    for s, part in enumerate(parts):
        source = lax.rem(me + (count - s), count)
        full[:, pl.ds(pl.multiple_of(source * width, LANES), width)] = part[...]


def send_kernel(count, paired, picked_ref, live_ref, lane_ref, keep_ref, *refs):
    parts, outs, masked_ref, full = refs[:count], refs[count:-2], refs[-2], refs[-1]
    stencil, cells = full.shape
    rows = picked_ref.shape[0] - SUB
    blocks, slots = len(outs), outs[0].shape[1]
    place_weights(parts, full)
    pad = jnp.zeros((SUB - stencil, LANES), F32)
    pieces = []
    for t in range(cells // LANES):
        pieces += [full[:, t * LANES : (t + 1) * LANES], pad]
    w = jnp.concatenate(pieces, axis=0)
    w0 = w.astype(BF16).astype(F32)
    w1 = (w - w0).astype(BF16).astype(F32)
    terms = jnp.concatenate([w0, w1, w - w0 - w1], axis=0).astype(BF16)
    got = jnp.dot(terms, lane_ref[...], preferred_element_type=F32)
    n = w.shape[0]
    got = (got[:n] + got[n : 2 * n] + got[2 * n :]) * live_ref[...].astype(F32)
    weight = jnp.sum(got, axis=0, keepdims=True)
    message = [
        jnp.concatenate(
            [picked_ref[:rows, j * slots : (j + 1) * slots] * weight[:, j * slots : (j + 1) * slots], picked_ref[rows:, j * slots : (j + 1) * slots]],
            axis=0,
        )
        for j in range(blocks)
    ]
    if paired:
        even = lax.rem(lax.axis_index("panel"), 2) == 0
        low, high, previous, following = message
        message = [
            jnp.where(even, high, low),
            jnp.where(even, low, high),
            jnp.where(even, following, previous),
            jnp.where(even, previous, following),
        ]
    for out, m in zip(outs, message):
        out[...] = m
    masked_ref[...] = full[...] * keep_ref[...]


def local_kernel(u_ref, dep_ref, w_ref, acc_ref):
    cells = u_ref.shape[1]
    acc_ref[...] = scatter_product(
        [
            (two_terms(u_ref[...] * w_ref[k : k + 1, :]).astype(BF16), dep_ref[k : k + 1, :])
            for k in range(dep_ref.shape[0])
        ],
        cells,
    )


def arrive_kernel(acc_ref, *refs):
    received, out_ref = refs[:-1], refs[-1]
    rows, cells = out_ref.shape
    values = jnp.concatenate([r[:rows, :] for r in received], axis=1)
    ids = jnp.concatenate([r[rows : rows + 1, :] for r in received], axis=1).astype(I32)
    sums = scatter_product([(two_terms(values).astype(BF16), ids)], cells)
    for h in range(cells // LO):
        a, b, c = (2 * h * rows + i * rows for i in range(3))
        out_ref[:, h * LO : (h + 1) * LO] = (acc_ref[a:b] + acc_ref[b:c]) + (sums[a:b] + sums[b:c])


def rotated(value, axis, steps):
    count = lax.axis_size(axis)
    return lax.ppermute(value, axis, [(i, (i + steps) % count) for i in range(count)])


def racetrack(value, reverse):
    sectors, tiles = lax.axis_size("panel"), lax.axis_size("tile")
    route = []
    for p in range(sectors):
        step = 1 if (p % 2 == 0) != reverse else -1
        for t in range(tiles):
            q, to = (p, t + step) if 0 <= t + step < tiles else (p ^ 1, t)
            route.append((p * tiles + t, q * tiles + to))
    return lax.ppermute(value, ("panel", "tile"), route)


def swapped(value, outer):
    count = lax.axis_size("panel")
    step = [1, -1] if not outer else [-1, 1]
    return lax.ppermute(value, "panel", [(i, (i + step[i % 2]) % count) for i in range(count)])


def body(adjoint_new, weights, departure, send_point, block_count, rotation):
    fields, levels, cells = adjoint_new.shape
    blocks, slots = send_point.shape
    stencil = departure.shape[0]
    rows = fields * levels
    count = lax.axis_size("lev")
    paired = lax.axis_size("panel") % 2 == 0
    points = blocks * slots
    shape = jax.ShapeDtypeStruct
    parts = [rotated(weights, "lev", s) for s in range(1, count)]
    inputs = (
        adjoint_new.reshape(rows, cells), weights, departure, send_point,
        block_count.reshape(1, -1), rotation.reshape(1, -1),
    )
    u, own, dep, keep, picked, live, lane = pl.pallas_call(
        lambda *refs: prepare_kernel(levels, *refs),
        out_shape=[
            shape((rows, cells), F32),
            shape(weights.shape, F32),
            shape((stencil, cells), I32),
            shape((stencil, cells), F32),
            shape((rows + SUB, points), F32),
            shape((cells // LANES * SUB, points), BF16),
            shape((LANES, points), BF16),
        ],
        in_specs=[HBM] * 6,
        out_specs=[VMEM] * 7,
        scratch_shapes=[
            pltpu.VMEM((blocks, slots), I32),
            pltpu.VMEM((1, block_count.size), I32),
            pltpu.VMEM((1, rotation.size), I32),
            pltpu.SemaphoreType.DMA((6,)),
        ],
        cost_estimate=pl.CostEstimate(
            flops=4 * rows * cells * points, bytes_accessed=8 * rows * cells, transcendentals=0
        ),
        compiler_params=PARAMS,
        name="prepare",
    )(*(pltpu.with_memory_space_constraint(a, pltpu.HBM) for a in inputs))
    block = shape((rows + SUB, slots), F32)
    *outgoing, masked = pl.pallas_call(
        lambda *refs: send_kernel(count, paired, *refs),
        out_shape=[block] * blocks + [shape((stencil, cells), F32)],
        in_specs=[VMEM] * (4 + count),
        out_specs=[VMEM] * (blocks + 1),
        scratch_shapes=[pltpu.VMEM((stencil, cells), F32)],
        compiler_params=PARAMS,
        name="send",
    )(picked, live, lane, keep, own, *parts)
    if paired:
        received = [
            racetrack(outgoing[0], False),
            racetrack(outgoing[1], True),
            swapped(outgoing[2], False),
            swapped(outgoing[3], True),
        ]
    else:
        received = [
            rotated(outgoing[1], "tile", 1),
            rotated(outgoing[0], "tile", -1),
            rotated(outgoing[3], "panel", 1),
            rotated(outgoing[2], "panel", -1),
        ]
    local = pl.pallas_call(
        local_kernel,
        out_shape=shape((cells // LO * 2 * rows, LO), F32),
        in_specs=[VMEM] * 3,
        out_specs=VMEM,
        cost_estimate=pl.CostEstimate(
            flops=4 * rows * cells * stencil * cells, bytes_accessed=8 * rows * cells, transcendentals=0
        ),
        compiler_params=PARAMS,
        name="local",
    )(u, dep, masked)
    out = pl.pallas_call(
        arrive_kernel,
        out_shape=shape((rows, cells), F32),
        in_specs=[VMEM] * (1 + blocks),
        out_specs=VMEM,
        compiler_params=PARAMS,
        name="arrive",
    )(local, *received)
    return out.reshape(fields, levels, cells)


def solution(mesh):
    return jax.shard_map(
        body,
        mesh=mesh,
        in_specs=(
            P(None, "lev", ("panel", "tile")),
            P(None, ("panel", "tile", "lev")),
            P(None, ("panel", "tile")),
            P(None, ("panel", "tile")),
            P(None, ("panel", "tile")),
            P(None, ("panel", "tile")),
        ),
        out_specs=P(None, "lev", ("panel", "tile")),
        check_vma=False,
    )
```

```python
import jax
import jax.numpy as jnp
from jax import lax
from jax.experimental import pallas as pl
from jax.experimental.pallas import tpu as pltpu
from jax.sharding import PartitionSpec as P

F32, BF16, I32 = jnp.float32, jnp.bfloat16, jnp.int32
LO = 256
LANES = 128
SUB = 8
VMEM = pl.BlockSpec(memory_space=pltpu.VMEM)
HBM = pl.BlockSpec(memory_space=pltpu.HBM)
PARAMS = pltpu.CompilerParams(vmem_limit_bytes=32 << 20)
NT = (((1,), (1,)), ((), ()))


def one_hot(rows, index):
    row = lax.broadcasted_iota(I32, (rows, index.shape[1]), 0)
    return (row == index).astype(F32).astype(BF16)


def two_terms(value):
    high = value.astype(BF16).astype(F32)
    return jnp.concatenate([high, value - high], axis=0)


def scatter_product(segments, cells):
    left = [[] for _ in range(cells // LO)]
    right = []
    for terms, target in segments:
        high = target // LO
        for h, row in enumerate(left):
            row.append(terms * (high == h).astype(F32).astype(BF16))
        right.append(one_hot(LO, target - high * LO))
    left = jnp.concatenate([jnp.concatenate(row, axis=1) for row in left], axis=0)
    return lax.dot_general(left, jnp.concatenate(right, axis=1), NT, preferred_element_type=F32)


def piece(steps, width):
    count = lax.axis_size("lev")
    source = lax.rem(lax.axis_index("lev") + (count - steps), count)
    return pl.ds(pl.multiple_of(source * width, LANES), width)


def scattered(u_ref, dep_ref, weight, k, at):
    return two_terms(u_ref[:, at] * weight).astype(BF16), dep_ref[k : k + 1, at]


def prepare_kernel(
    levels, early, u_hbm, w_hbm, dep_hbm, sp_hbm, bc_hbm, rot_hbm,
    u_ref, w_ref, dep_ref, keep_ref, picked_ref, live_ref, lane_ref, acc_ref,
    sp_ref, bc_ref, rot_ref, sems,
):
    pairs = [(sp_hbm, sp_ref), (bc_hbm, bc_ref), (rot_hbm, rot_ref), (dep_hbm, dep_ref), (u_hbm, u_ref), (w_hbm, w_ref)]
    copies = [pltpu.make_async_copy(a, b, sems.at[i]) for i, (a, b) in enumerate(pairs)]
    for c in copies:
        c.start()
    for c in copies[:3]:
        c.wait()
    rows, cells = u_ref.shape
    stencil = dep_ref.shape[0]
    blocks, slots = sp_ref.shape
    tiles = cells // LANES
    slot = lax.broadcasted_iota(I32, (1, slots), 1)
    which, columns, codes, lanes = [], [], [], []
    for j in range(blocks):
        chosen = sp_ref[j : j + 1, :]
        k = chosen // cells
        column = chosen - k * cells
        tile = column // LANES
        which.append(k)
        columns.append(column)
        codes.append(jnp.where(slot < bc_ref[0:1, j : j + 1], tile * SUB + k, -1))
        lanes.append(column - tile * LANES)
    live = one_hot(tiles * SUB, jnp.concatenate(codes, axis=1))
    lane = one_hot(LANES, jnp.concatenate(lanes, axis=1))
    live_ref[...] = live
    lane_ref[...] = lane
    sent = lax.dot_general(live, lane, NT, preferred_element_type=F32)
    for t in range(tiles):
        keep_ref[:, t * LANES : (t + 1) * LANES] = 1.0 - sent[t * SUB : t * SUB + stencil]
    for c in copies[3:]:
        c.wait()
    dep = dep_ref[...]
    dep_high = dep // SUB
    dep_low = dep - dep_high * SUB
    table = jnp.concatenate(
        [two_terms(u_ref[...]), jnp.concatenate([dep_high.astype(F32), dep_low.astype(F32)], axis=0), jnp.zeros((SUB, cells), F32)],
        axis=0,
    ).astype(BF16)
    onehot = one_hot(cells, jnp.concatenate(columns, axis=1))
    got = jnp.dot(table, onehot, preferred_element_type=F32)
    at = 2 * rows
    for j in range(blocks):
        here = slice(j * slots, (j + 1) * slots)
        g = got[:, here]
        ids = jnp.zeros((1, slots), F32)
        for k in range(stencil):
            one_id = g[at + k : at + k + 1] * SUB + g[at + stencil + k : at + stencil + k + 1]
            ids = ids + jnp.where(which[j] == k, one_id, 0.0)
        values = g[:rows] + g[rows : 2 * rows]
        zonal, merid = values[:levels], values[levels : 2 * levels]
        if j >= 2:
            code = rot_ref[0:1, j - 2 : j - 1]
            cosine = (code == 0).astype(F32) - (code == 2).astype(F32)
            sine = (code == 1).astype(F32) - (code == 3).astype(F32)
            zonal, merid = cosine * zonal + sine * merid, cosine * merid - sine * zonal
        picked_ref[:levels, here] = zonal
        picked_ref[levels : 2 * levels, here] = merid
        picked_ref[2 * levels : rows, here] = values[2 * levels :]
        picked_ref[rows:, here] = jnp.broadcast_to(ids, (SUB, slots))
    own = piece(0, w_ref.shape[1])
    acc_ref[...] = scatter_product(
        [scattered(u_ref, dep_ref, w_ref[k : k + 1, :] * keep_ref[k : k + 1, own], k, own) for k in range(early)], cells
    )


def send_kernel(count, paired, picked_ref, live_ref, lane_ref, keep_ref, *refs):
    parts, outs, masked_ref, full = refs[:count], refs[count:-2], refs[-2], refs[-1]
    stencil, cells = full.shape
    rows = picked_ref.shape[0] - SUB
    blocks, slots = len(outs), outs[0].shape[1]
    for steps, part in enumerate(parts):
        full[:, piece(steps, part.shape[1])] = part[...]
    pad = jnp.zeros((SUB - stencil, LANES), F32)
    pieces = []
    for t in range(cells // LANES):
        pieces += [full[:, t * LANES : (t + 1) * LANES], pad]
    w = jnp.concatenate(pieces, axis=0)
    w0 = w.astype(BF16).astype(F32)
    w1 = (w - w0).astype(BF16).astype(F32)
    terms = jnp.concatenate([w0, w1, w - w0 - w1], axis=0).astype(BF16)
    got = jnp.dot(terms, lane_ref[...], preferred_element_type=F32)
    n = w.shape[0]
    got = (got[:n] + got[n : 2 * n] + got[2 * n :]) * live_ref[...].astype(F32)
    weight = jnp.sum(got, axis=0, keepdims=True)
    message = [
        jnp.concatenate(
            [picked_ref[:rows, j * slots : (j + 1) * slots] * weight[:, j * slots : (j + 1) * slots], picked_ref[rows:, j * slots : (j + 1) * slots]],
            axis=0,
        )
        for j in range(blocks)
    ]
    if paired:
        even = lax.rem(lax.axis_index("panel"), 2) == 0
        low, high, previous, following = message
        message = [
            jnp.where(even, high, low),
            jnp.where(even, low, high),
            jnp.where(even, following, previous),
            jnp.where(even, previous, following),
        ]
    for out, m in zip(outs, message):
        out[...] = m
    masked_ref[...] = full[...] * keep_ref[...]


def local_kernel(early, count, u_ref, dep_ref, w_ref, early_ref, acc_ref):
    stencil, cells = dep_ref.shape
    at = [(k, piece(s, cells // count)) for k in range(early) for s in range(1, count)]
    at += [(k, slice(None)) for k in range(early, stencil)]
    acc_ref[...] = early_ref[...] + scatter_product(
        [scattered(u_ref, dep_ref, w_ref[k : k + 1, here], k, here) for k, here in at], cells
    )


def arrive_kernel(acc_ref, *refs):
    received, out_ref = refs[:-1], refs[-1]
    rows, cells = out_ref.shape
    values = jnp.concatenate([r[:rows, :] for r in received], axis=1)
    ids = jnp.concatenate([r[rows : rows + 1, :] for r in received], axis=1).astype(I32)
    sums = scatter_product([(two_terms(values).astype(BF16), ids)], cells)
    for h in range(cells // LO):
        a, b, c = (2 * h * rows + i * rows for i in range(3))
        out_ref[:, h * LO : (h + 1) * LO] = (acc_ref[a:b] + acc_ref[b:c]) + (sums[a:b] + sums[b:c])


def rotated(value, axis, steps):
    count = lax.axis_size(axis)
    return lax.ppermute(value, axis, [(i, (i + steps) % count) for i in range(count)])


def racetrack(value, reverse):
    sectors, tiles = lax.axis_size("panel"), lax.axis_size("tile")
    route = []
    for p in range(sectors):
        step = 1 if (p % 2 == 0) != reverse else -1
        for t in range(tiles):
            q, to = (p, t + step) if 0 <= t + step < tiles else (p ^ 1, t)
            route.append((p * tiles + t, q * tiles + to))
    return lax.ppermute(value, ("panel", "tile"), route)


def swapped(value, outer):
    count = lax.axis_size("panel")
    step = [1, -1] if not outer else [-1, 1]
    return lax.ppermute(value, "panel", [(i, (i + step[i % 2]) % count) for i in range(count)])


def body(adjoint_new, weights, departure, send_point, block_count, rotation):
    fields, levels, cells = adjoint_new.shape
    blocks, slots = send_point.shape
    stencil = departure.shape[0]
    rows = fields * levels
    count = lax.axis_size("lev")
    paired = lax.axis_size("panel") % 2 == 0
    points = blocks * slots
    early = stencil // 2
    shape = jax.ShapeDtypeStruct
    parts = [rotated(weights, "lev", s) for s in range(1, count)]
    inputs = (
        adjoint_new.reshape(rows, cells), weights, departure, send_point,
        block_count.reshape(1, -1), rotation.reshape(1, -1),
    )
    sums = shape((cells // LO * 2 * rows, LO), F32)
    u, own, dep, keep, picked, live, lane, acc = pl.pallas_call(
        lambda *refs: prepare_kernel(levels, early, *refs),
        out_shape=[
            shape((rows, cells), F32),
            shape(weights.shape, F32),
            shape((stencil, cells), I32),
            shape((stencil, cells), F32),
            shape((rows + SUB, points), F32),
            shape((cells // LANES * SUB, points), BF16),
            shape((LANES, points), BF16),
            sums,
        ],
        in_specs=[HBM] * 6,
        out_specs=[VMEM] * 8,
        scratch_shapes=[
            pltpu.VMEM((blocks, slots), I32),
            pltpu.VMEM((1, block_count.size), I32),
            pltpu.VMEM((1, rotation.size), I32),
            pltpu.SemaphoreType.DMA((6,)),
        ],
        cost_estimate=pl.CostEstimate(
            flops=4 * rows * cells * points, bytes_accessed=8 * rows * cells, transcendentals=0
        ),
        compiler_params=PARAMS,
        name="prepare",
    )(*(pltpu.with_memory_space_constraint(a, pltpu.HBM) for a in inputs))
    block = shape((rows + SUB, slots), F32)
    *outgoing, masked = pl.pallas_call(
        lambda *refs: send_kernel(count, paired, *refs),
        out_shape=[block] * blocks + [shape((stencil, cells), F32)],
        in_specs=[VMEM] * (4 + count),
        out_specs=[VMEM] * (blocks + 1),
        scratch_shapes=[pltpu.VMEM((stencil, cells), F32)],
        compiler_params=PARAMS,
        name="send",
    )(picked, live, lane, keep, own, *parts)
    if paired:
        received = [
            racetrack(outgoing[0], False),
            racetrack(outgoing[1], True),
            swapped(outgoing[2], False),
            swapped(outgoing[3], True),
        ]
    else:
        received = [
            rotated(outgoing[1], "tile", 1),
            rotated(outgoing[0], "tile", -1),
            rotated(outgoing[3], "panel", 1),
            rotated(outgoing[2], "panel", -1),
        ]
    local = pl.pallas_call(
        lambda *refs: local_kernel(early, count, *refs),
        out_shape=sums,
        in_specs=[VMEM] * 4,
        out_specs=VMEM,
        cost_estimate=pl.CostEstimate(
            flops=4 * rows * cells * stencil * cells, bytes_accessed=8 * rows * cells, transcendentals=0
        ),
        compiler_params=PARAMS,
        name="local",
    )(u, dep, masked, acc)
    out = pl.pallas_call(
        arrive_kernel,
        out_shape=shape((rows, cells), F32),
        in_specs=[VMEM] * (1 + blocks),
        out_specs=VMEM,
        compiler_params=PARAMS,
        name="arrive",
    )(local, *received)
    return out.reshape(fields, levels, cells)


def solution(mesh):
    return jax.shard_map(
        body,
        mesh=mesh,
        in_specs=(
            P(None, "lev", ("panel", "tile")),
            P(None, ("panel", "tile", "lev")),
            P(None, ("panel", "tile")),
            P(None, ("panel", "tile")),
            P(None, ("panel", "tile")),
            P(None, ("panel", "tile")),
        ),
        out_specs=P(None, "lev", ("panel", "tile")),
        check_vma=False,
    )
```

```python
import jax
import jax.numpy as jnp
from jax import lax
from jax.experimental import pallas as pl
from jax.experimental.pallas import tpu as pltpu
from jax.sharding import PartitionSpec as P

F32, BF16, I32 = jnp.float32, jnp.bfloat16, jnp.int32
LO = 256
LANES = 128
SUB = 8
VMEM = pl.BlockSpec(memory_space=pltpu.VMEM)
HBM = pl.BlockSpec(memory_space=pltpu.HBM)
PARAMS = pltpu.CompilerParams(vmem_limit_bytes=32 << 20)
NT = (((1,), (1,)), ((), ()))


def one_hot(rows, index):
    row = lax.broadcasted_iota(I32, (rows, index.shape[1]), 0)
    return (row == index).astype(F32).astype(BF16)


def two_terms(value):
    high = value.astype(BF16).astype(F32)
    return jnp.concatenate([high, value - high], axis=0)


def scatter_product(segments, cells):
    left = [[] for _ in range(cells // LO)]
    right = []
    for terms, target in segments:
        high = target // LO
        for h, row in enumerate(left):
            row.append(terms * (high == h).astype(F32).astype(BF16))
        right.append(one_hot(LO, target - high * LO))
    left = jnp.concatenate([jnp.concatenate(row, axis=1) for row in left], axis=0)
    return lax.dot_general(left, jnp.concatenate(right, axis=1), NT, preferred_element_type=F32)


def piece(steps, width):
    count = lax.axis_size("lev")
    source = lax.rem(lax.axis_index("lev") + (count - steps), count)
    return pl.ds(pl.multiple_of(source * width, LANES), width)


def scattered(u_ref, dep_ref, weight, k, at):
    return two_terms(u_ref[:, at] * weight).astype(BF16), dep_ref[k : k + 1, at]


def prepare_kernel(
    levels, early, u_hbm, w_hbm, dep_hbm, sp_hbm, bc_hbm, rot_hbm,
    u_ref, w_ref, dep_ref, keep_ref, picked_ref, live_ref, lane_ref, acc_ref,
    sp_ref, bc_ref, rot_ref, sems,
):
    pairs = [(sp_hbm, sp_ref), (bc_hbm, bc_ref), (rot_hbm, rot_ref), (dep_hbm, dep_ref), (u_hbm, u_ref), (w_hbm, w_ref)]
    copies = [pltpu.make_async_copy(a, b, sems.at[i]) for i, (a, b) in enumerate(pairs)]
    for c in copies:
        c.start()
    for c in copies[:3]:
        c.wait()
    rows, cells = u_ref.shape
    stencil = dep_ref.shape[0]
    blocks, slots = sp_ref.shape
    tiles = cells // LANES
    slot = lax.broadcasted_iota(I32, (1, slots), 1)
    which, columns, codes, lanes = [], [], [], []
    for j in range(blocks):
        chosen = sp_ref[j : j + 1, :]
        k = chosen // cells
        column = chosen - k * cells
        tile = column // LANES
        which.append(k)
        columns.append(column)
        codes.append(jnp.where(slot < bc_ref[0:1, j : j + 1], tile * SUB + k, -1))
        lanes.append(column - tile * LANES)
    live = one_hot(tiles * SUB, jnp.concatenate(codes, axis=1))
    lane = one_hot(LANES, jnp.concatenate(lanes, axis=1))
    live_ref[...] = live
    lane_ref[...] = lane
    sent = lax.dot_general(live, lane, NT, preferred_element_type=F32)
    for t in range(tiles):
        keep_ref[:, t * LANES : (t + 1) * LANES] = 1.0 - sent[t * SUB : t * SUB + stencil]
    for c in copies[3:]:
        c.wait()
    dep = dep_ref[...]
    dep_high = dep // SUB
    dep_low = dep - dep_high * SUB
    table = jnp.concatenate(
        [two_terms(u_ref[...]), dep_high.astype(F32), dep_low.astype(F32), jnp.zeros((SUB, cells), F32)],
        axis=0,
    ).astype(BF16)
    column = jnp.concatenate(columns, axis=1)
    chunk = column // LO
    height = table.shape[0]
    got = jnp.dot(
        jnp.concatenate([table[:, c * LO : (c + 1) * LO] for c in range(cells // LO)], axis=0),
        one_hot(LO, column - chunk * LO),
        preferred_element_type=F32,
    )
    values = jnp.zeros((rows, blocks * slots), F32)
    targets = jnp.zeros((2 * stencil, blocks * slots), F32)
    for c in range(cells // LO):
        at = c * height
        here = chunk == c
        values = values + jnp.where(here, got[at : at + rows] + got[at + rows : at + 2 * rows], 0.0)
        targets = targets + jnp.where(here, got[at + 2 * rows : at + 2 * rows + 2 * stencil], 0.0)
    k = jnp.concatenate(which, axis=1)
    ids = jnp.zeros((1, blocks * slots), F32)
    for i in range(stencil):
        ids = ids + jnp.where(k == i, targets[i : i + 1] * SUB + targets[stencil + i : stencil + i + 1], 0.0)
    picked_ref[rows:, :] = jnp.broadcast_to(ids, (SUB, blocks * slots))
    picked_ref[2 * levels : rows, :] = values[2 * levels :]
    for j in range(blocks):
        here = slice(j * slots, (j + 1) * slots)
        zonal, merid = values[:levels, here], values[levels : 2 * levels, here]
        if j >= 2:
            code = rot_ref[0:1, j - 2 : j - 1]
            cosine = (code == 0).astype(F32) - (code == 2).astype(F32)
            sine = (code == 1).astype(F32) - (code == 3).astype(F32)
            zonal, merid = cosine * zonal + sine * merid, cosine * merid - sine * zonal
        picked_ref[:levels, here] = zonal
        picked_ref[levels : 2 * levels, here] = merid
    own = piece(0, w_ref.shape[1])
    acc_ref[...] = scatter_product(
        [scattered(u_ref, dep_ref, w_ref[k : k + 1, :] * keep_ref[k : k + 1, own], k, own) for k in range(early)], cells
    )


def send_kernel(count, paired, picked_ref, live_ref, lane_ref, keep_ref, *refs):
    parts, outs, masked_ref, full = refs[:count], refs[count:-2], refs[-2], refs[-1]
    stencil, cells = full.shape
    rows = picked_ref.shape[0] - SUB
    blocks, slots = len(outs), outs[0].shape[1]
    for steps, part in enumerate(parts):
        full[:, piece(steps, part.shape[1])] = part[...]
    pad = jnp.zeros((SUB - stencil, LANES), F32)
    pieces = []
    for t in range(cells // LANES):
        pieces += [full[:, t * LANES : (t + 1) * LANES], pad]
    w = jnp.concatenate(pieces, axis=0)
    w0 = w.astype(BF16).astype(F32)
    w1 = (w - w0).astype(BF16).astype(F32)
    terms = jnp.concatenate([w0, w1, w - w0 - w1], axis=0).astype(BF16)
    got = jnp.dot(terms, lane_ref[...], preferred_element_type=F32)
    n = w.shape[0]
    got = (got[:n] + got[n : 2 * n] + got[2 * n :]) * live_ref[...].astype(F32)
    weight = jnp.sum(got, axis=0, keepdims=True)
    message = [
        jnp.concatenate(
            [picked_ref[:rows, j * slots : (j + 1) * slots] * weight[:, j * slots : (j + 1) * slots], picked_ref[rows:, j * slots : (j + 1) * slots]],
            axis=0,
        )
        for j in range(blocks)
    ]
    if paired:
        even = lax.rem(lax.axis_index("panel"), 2) == 0
        low, high, previous, following = message
        message = [
            jnp.where(even, high, low),
            jnp.where(even, low, high),
            jnp.where(even, following, previous),
            jnp.where(even, previous, following),
        ]
    for out, m in zip(outs, message):
        out[...] = m
    masked_ref[...] = full[...] * keep_ref[...]


def local_kernel(early, count, u_ref, dep_ref, w_ref, early_ref, acc_ref):
    stencil, cells = dep_ref.shape
    at = [(k, piece(s, cells // count)) for k in range(early) for s in range(1, count)]
    at += [(k, slice(None)) for k in range(early, stencil)]
    acc_ref[...] = early_ref[...] + scatter_product(
        [scattered(u_ref, dep_ref, w_ref[k : k + 1, here], k, here) for k, here in at], cells
    )


def arrive_kernel(acc_ref, *refs):
    received, out_ref = refs[:-1], refs[-1]
    rows, cells = out_ref.shape
    values = jnp.concatenate([r[:rows, :] for r in received], axis=1)
    ids = jnp.concatenate([r[rows : rows + 1, :] for r in received], axis=1).astype(I32)
    sums = scatter_product([(two_terms(values).astype(BF16), ids)], cells)
    for h in range(cells // LO):
        a, b, c = (2 * h * rows + i * rows for i in range(3))
        out_ref[:, h * LO : (h + 1) * LO] = (acc_ref[a:b] + acc_ref[b:c]) + (sums[a:b] + sums[b:c])


def rotated(value, axis, steps):
    count = lax.axis_size(axis)
    return lax.ppermute(value, axis, [(i, (i + steps) % count) for i in range(count)])


def racetrack(value, reverse):
    sectors, tiles = lax.axis_size("panel"), lax.axis_size("tile")
    route = []
    for p in range(sectors):
        step = 1 if (p % 2 == 0) != reverse else -1
        for t in range(tiles):
            q, to = (p, t + step) if 0 <= t + step < tiles else (p ^ 1, t)
            route.append((p * tiles + t, q * tiles + to))
    return lax.ppermute(value, ("panel", "tile"), route)


def swapped(value, outer):
    count = lax.axis_size("panel")
    step = [1, -1] if not outer else [-1, 1]
    return lax.ppermute(value, "panel", [(i, (i + step[i % 2]) % count) for i in range(count)])


def body(adjoint_new, weights, departure, send_point, block_count, rotation):
    fields, levels, cells = adjoint_new.shape
    blocks, slots = send_point.shape
    stencil = departure.shape[0]
    rows = fields * levels
    count = lax.axis_size("lev")
    paired = lax.axis_size("panel") % 2 == 0
    points = blocks * slots
    early = stencil // 2
    shape = jax.ShapeDtypeStruct
    parts = [rotated(weights, "lev", s) for s in range(1, count)]
    inputs = (
        adjoint_new.reshape(rows, cells), weights, departure, send_point,
        block_count.reshape(1, -1), rotation.reshape(1, -1),
    )
    sums = shape((cells // LO * 2 * rows, LO), F32)
    u, own, dep, keep, picked, live, lane, acc = pl.pallas_call(
        lambda *refs: prepare_kernel(levels, early, *refs),
        out_shape=[
            shape((rows, cells), F32),
            shape(weights.shape, F32),
            shape((stencil, cells), I32),
            shape((stencil, cells), F32),
            shape((rows + SUB, points), F32),
            shape((cells // LANES * SUB, points), BF16),
            shape((LANES, points), BF16),
            sums,
        ],
        in_specs=[HBM] * 6,
        out_specs=[VMEM] * 8,
        scratch_shapes=[
            pltpu.VMEM((blocks, slots), I32),
            pltpu.VMEM((1, block_count.size), I32),
            pltpu.VMEM((1, rotation.size), I32),
            pltpu.SemaphoreType.DMA((6,)),
        ],
        cost_estimate=pl.CostEstimate(
            flops=4 * rows * cells * points, bytes_accessed=8 * rows * cells, transcendentals=0
        ),
        compiler_params=PARAMS,
        name="prepare",
    )(*(pltpu.with_memory_space_constraint(a, pltpu.HBM) for a in inputs))
    block = shape((rows + SUB, slots), F32)
    *outgoing, masked = pl.pallas_call(
        lambda *refs: send_kernel(count, paired, *refs),
        out_shape=[block] * blocks + [shape((stencil, cells), F32)],
        in_specs=[VMEM] * (4 + count),
        out_specs=[VMEM] * (blocks + 1),
        scratch_shapes=[pltpu.VMEM((stencil, cells), F32)],
        compiler_params=PARAMS,
        name="send",
    )(picked, live, lane, keep, own, *parts)
    if paired:
        received = [
            swapped(outgoing[3], True),
            racetrack(outgoing[1], True),
            racetrack(outgoing[0], False),
            swapped(outgoing[2], False),
        ]
    else:
        received = [
            rotated(outgoing[1], "tile", 1),
            rotated(outgoing[0], "tile", -1),
            rotated(outgoing[3], "panel", 1),
            rotated(outgoing[2], "panel", -1),
        ]
    local = pl.pallas_call(
        lambda *refs: local_kernel(early, count, *refs),
        out_shape=sums,
        in_specs=[VMEM] * 4,
        out_specs=VMEM,
        cost_estimate=pl.CostEstimate(
            flops=4 * rows * cells * stencil * cells, bytes_accessed=8 * rows * cells, transcendentals=0
        ),
        compiler_params=PARAMS,
        name="local",
    )(u, dep, masked, acc)
    out = pl.pallas_call(
        arrive_kernel,
        out_shape=shape((rows, cells), F32),
        in_specs=[VMEM] * (1 + blocks),
        out_specs=VMEM,
        compiler_params=PARAMS,
        name="arrive",
    )(local, *received)
    return out.reshape(fields, levels, cells)


def solution(mesh):
    return jax.shard_map(
        body,
        mesh=mesh,
        in_specs=(
            P(None, "lev", ("panel", "tile")),
            P(None, ("panel", "tile", "lev")),
            P(None, ("panel", "tile")),
            P(None, ("panel", "tile")),
            P(None, ("panel", "tile")),
            P(None, ("panel", "tile")),
        ),
        out_specs=P(None, "lev", ("panel", "tile")),
        check_vma=False,
    )
```

```python
import jax
import jax.numpy as jnp
from jax import lax
from jax.experimental import pallas as pl
from jax.experimental.pallas import tpu as pltpu
from jax.sharding import PartitionSpec as P

F32, BF16, I32 = jnp.float32, jnp.bfloat16, jnp.int32
LO = 256
LANES = 128
SUB = 8
VMEM = pl.BlockSpec(memory_space=pltpu.VMEM)
HBM = pl.BlockSpec(memory_space=pltpu.HBM)
PARAMS = pltpu.CompilerParams(vmem_limit_bytes=32 << 20)
NT = (((1,), (1,)), ((), ()))


def one_hot(rows, index):
    row = lax.broadcasted_iota(I32, (rows, index.shape[1]), 0)
    return (row == index).astype(F32).astype(BF16)


def two_terms(value):
    high = value.astype(BF16).astype(F32)
    return jnp.concatenate([high, value - high], axis=0)


def scatter_product(segments, cells):
    left = [[] for _ in range(cells // LO)]
    right = []
    for terms, target in segments:
        high = target // LO
        for h, row in enumerate(left):
            row.append(terms * (high == h).astype(F32).astype(BF16))
        right.append(one_hot(LO, target - high * LO))
    left = jnp.concatenate([jnp.concatenate(row, axis=1) for row in left], axis=0)
    return lax.dot_general(left, jnp.concatenate(right, axis=1), NT, preferred_element_type=F32)


def piece(steps, width):
    count = lax.axis_size("lev")
    source = lax.rem(lax.axis_index("lev") + (count - steps), count)
    return pl.ds(pl.multiple_of(source * width, LANES), width)


def scattered(u_ref, dep_ref, weight, k, at):
    return two_terms(u_ref[:, at] * weight).astype(BF16), dep_ref[k : k + 1, at]


def prepare_kernel(
    levels, early, u_hbm, w_hbm, dep_hbm, sp_hbm, bc_hbm, rot_hbm,
    u_ref, w_ref, dep_ref, keep_ref, picked_ref, live_ref, lane_ref, acc_ref,
    sp_ref, bc_ref, rot_ref, sems,
):
    pairs = [(sp_hbm, sp_ref), (bc_hbm, bc_ref), (rot_hbm, rot_ref), (dep_hbm, dep_ref), (u_hbm, u_ref), (w_hbm, w_ref)]
    copies = [pltpu.make_async_copy(a, b, sems.at[i]) for i, (a, b) in enumerate(pairs)]
    for c in copies:
        c.start()
    for c in copies[:3]:
        c.wait()
    rows, cells = u_ref.shape
    stencil = dep_ref.shape[0]
    blocks, slots = sp_ref.shape
    tiles = cells // LANES
    slot = lax.broadcasted_iota(I32, (1, slots), 1)
    which, columns, codes, lanes = [], [], [], []
    for j in range(blocks):
        chosen = sp_ref[j : j + 1, :]
        k = chosen // cells
        column = chosen - k * cells
        tile = column // LANES
        which.append(k)
        columns.append(column)
        codes.append(jnp.where(slot < bc_ref[0:1, j : j + 1], tile * SUB + k, -1))
        lanes.append(column - tile * LANES)
    live = one_hot(tiles * SUB, jnp.concatenate(codes, axis=1))
    lane = one_hot(LANES, jnp.concatenate(lanes, axis=1))
    live_ref[...] = live
    lane_ref[...] = lane
    sent = lax.dot_general(live, lane, NT, preferred_element_type=F32)
    for t in range(tiles):
        keep_ref[:, t * LANES : (t + 1) * LANES] = 1.0 - sent[t * SUB : t * SUB + stencil]
    for c in copies[3:]:
        c.wait()
    dep = dep_ref[...]
    dep_high = dep // SUB
    dep_low = dep - dep_high * SUB
    table = jnp.concatenate(
        [two_terms(u_ref[...]), dep_high.astype(F32), dep_low.astype(F32), jnp.zeros((SUB, cells), F32)],
        axis=0,
    ).astype(BF16)
    column = jnp.concatenate(columns, axis=1)
    chunk = column // LO
    height = table.shape[0]
    got = jnp.dot(
        jnp.concatenate([table[:, c * LO : (c + 1) * LO] for c in range(cells // LO)], axis=0),
        one_hot(LO, column - chunk * LO),
        preferred_element_type=F32,
    )
    values = jnp.zeros((rows, blocks * slots), F32)
    targets = jnp.zeros((2 * stencil, blocks * slots), F32)
    for c in range(cells // LO):
        at = c * height
        here = chunk == c
        values = values + jnp.where(here, got[at : at + rows] + got[at + rows : at + 2 * rows], 0.0)
        targets = targets + jnp.where(here, got[at + 2 * rows : at + 2 * rows + 2 * stencil], 0.0)
    k = jnp.concatenate(which, axis=1)
    ids = jnp.zeros((1, blocks * slots), F32)
    for i in range(stencil):
        ids = ids + jnp.where(k == i, targets[i : i + 1] * SUB + targets[stencil + i : stencil + i + 1], 0.0)
    picked_ref[rows:, :] = jnp.broadcast_to(ids, (SUB, blocks * slots))
    picked_ref[2 * levels : rows, :] = values[2 * levels :]
    for j in range(blocks):
        here = slice(j * slots, (j + 1) * slots)
        zonal, merid = values[:levels, here], values[levels : 2 * levels, here]
        if j >= 2:
            code = rot_ref[0:1, j - 2 : j - 1]
            cosine = (code == 0).astype(F32) - (code == 2).astype(F32)
            sine = (code == 1).astype(F32) - (code == 3).astype(F32)
            zonal, merid = cosine * zonal + sine * merid, cosine * merid - sine * zonal
        picked_ref[:levels, here] = zonal
        picked_ref[levels : 2 * levels, here] = merid
    own = piece(0, w_ref.shape[1])
    acc_ref[...] = scatter_product(
        [scattered(u_ref, dep_ref, w_ref[k : k + 1, :] * keep_ref[k : k + 1, own], k, own) for k in range(early)], cells
    )


def send_kernel(count, paired, picked_ref, live_ref, lane_ref, keep_ref, *refs):
    parts, outs, masked_ref, full = refs[:count], refs[count:-2], refs[-2], refs[-1]
    stencil, cells = full.shape
    rows = picked_ref.shape[0] - SUB
    blocks, slots = len(outs), outs[0].shape[1]
    for steps, part in enumerate(parts):
        full[:, piece(steps, part.shape[1])] = part[...]
    pad = jnp.zeros((SUB - stencil, LANES), F32)
    pieces = []
    for t in range(cells // LANES):
        pieces += [full[:, t * LANES : (t + 1) * LANES], pad]
    w = jnp.concatenate(pieces, axis=0)
    w0 = w.astype(BF16).astype(F32)
    w1 = (w - w0).astype(BF16).astype(F32)
    terms = jnp.concatenate([w0, w1, w - w0 - w1], axis=0).astype(BF16)
    got = jnp.dot(terms, lane_ref[...], preferred_element_type=F32)
    n = w.shape[0]
    got = (got[:n] + got[n : 2 * n] + got[2 * n :]) * live_ref[...].astype(F32)
    weight = jnp.sum(got, axis=0, keepdims=True)
    message = [
        jnp.concatenate(
            [picked_ref[:rows, j * slots : (j + 1) * slots] * weight[:, j * slots : (j + 1) * slots], picked_ref[rows:, j * slots : (j + 1) * slots]],
            axis=0,
        )
        for j in range(blocks)
    ]
    low, high, previous, following = message
    if paired:
        even = lax.rem(lax.axis_index("panel"), 2) == 0
        low, high = jnp.where(even, low, high), jnp.where(even, high, low)
    message = [low, following, high, previous]
    for out, m in zip(outs, message):
        out[...] = m
    masked_ref[...] = full[...] * keep_ref[...]


def local_kernel(early, count, u_ref, dep_ref, w_ref, early_ref, acc_ref):
    stencil, cells = dep_ref.shape
    at = [(k, piece(s, cells // count)) for k in range(early) for s in range(1, count)]
    at += [(k, slice(None)) for k in range(early, stencil)]
    acc_ref[...] = early_ref[...] + scatter_product(
        [scattered(u_ref, dep_ref, w_ref[k : k + 1, here], k, here) for k, here in at], cells
    )


def arrive_kernel(acc_ref, *refs):
    received, out_ref = refs[:-1], refs[-1]
    rows, cells = out_ref.shape
    values = jnp.concatenate([r[:rows, :] for r in received], axis=1)
    ids = jnp.concatenate([r[rows : rows + 1, :] for r in received], axis=1).astype(I32)
    sums = scatter_product([(two_terms(values).astype(BF16), ids)], cells)
    for h in range(cells // LO):
        a, b, c = (2 * h * rows + i * rows for i in range(3))
        out_ref[:, h * LO : (h + 1) * LO] = (acc_ref[a:b] + acc_ref[b:c]) + (sums[a:b] + sums[b:c])


def rotated(value, axis, steps):
    count = lax.axis_size(axis)
    return lax.ppermute(value, axis, [(i, (i + steps) % count) for i in range(count)])


def racetrack(value, reverse):
    sectors, tiles = lax.axis_size("panel"), lax.axis_size("tile")
    route = []
    for p in range(sectors):
        step = 1 if (p % 2 == 0) != reverse else -1
        for t in range(tiles):
            q, to = (p, t + step) if 0 <= t + step < tiles else (p ^ 1, t)
            route.append((p * tiles + t, q * tiles + to))
    return lax.ppermute(value, ("panel", "tile"), route)


def body(adjoint_new, weights, departure, send_point, block_count, rotation):
    fields, levels, cells = adjoint_new.shape
    blocks, slots = send_point.shape
    stencil = departure.shape[0]
    rows = fields * levels
    count = lax.axis_size("lev")
    paired = lax.axis_size("panel") % 2 == 0
    points = blocks * slots
    early = 1
    shape = jax.ShapeDtypeStruct
    parts = [rotated(weights, "lev", s) for s in range(1, count)]
    inputs = (
        adjoint_new.reshape(rows, cells), weights, departure, send_point,
        block_count.reshape(1, -1), rotation.reshape(1, -1),
    )
    sums = shape((cells // LO * 2 * rows, LO), F32)
    u, own, dep, keep, picked, live, lane, acc = pl.pallas_call(
        lambda *refs: prepare_kernel(levels, early, *refs),
        out_shape=[
            shape((rows, cells), F32),
            shape(weights.shape, F32),
            shape((stencil, cells), I32),
            shape((stencil, cells), F32),
            shape((rows + SUB, points), F32),
            shape((cells // LANES * SUB, points), BF16),
            shape((LANES, points), BF16),
            sums,
        ],
        in_specs=[HBM] * 6,
        out_specs=[VMEM] * 8,
        scratch_shapes=[
            pltpu.VMEM((blocks, slots), I32),
            pltpu.VMEM((1, block_count.size), I32),
            pltpu.VMEM((1, rotation.size), I32),
            pltpu.SemaphoreType.DMA((6,)),
        ],
        cost_estimate=pl.CostEstimate(
            flops=4 * rows * cells * points, bytes_accessed=8 * rows * cells, transcendentals=0
        ),
        compiler_params=PARAMS,
        name="prepare",
    )(*(pltpu.with_memory_space_constraint(a, pltpu.HBM) for a in inputs))
    block = shape((rows + SUB, slots), F32)
    *outgoing, masked = pl.pallas_call(
        lambda *refs: send_kernel(count, paired, *refs),
        out_shape=[block] * blocks + [shape((stencil, cells), F32)],
        in_specs=[VMEM] * (4 + count),
        out_specs=[VMEM] * (blocks + 1),
        scratch_shapes=[pltpu.VMEM((stencil, cells), F32)],
        compiler_params=PARAMS,
        name="send",
    )(picked, live, lane, keep, own, *parts)
    if paired:
        back, forth = (lambda v: racetrack(v, True)), (lambda v: racetrack(v, False))
    else:
        back, forth = (lambda v: rotated(v, "tile", -1)), (lambda v: rotated(v, "tile", 1))
    received = [
        back(outgoing[0]),
        rotated(outgoing[1], "panel", 1),
        forth(outgoing[2]),
        rotated(outgoing[3], "panel", -1),
    ]
    local = pl.pallas_call(
        lambda *refs: local_kernel(early, count, *refs),
        out_shape=sums,
        in_specs=[VMEM] * 4,
        out_specs=VMEM,
        cost_estimate=pl.CostEstimate(
            flops=4 * rows * cells * stencil * cells, bytes_accessed=8 * rows * cells, transcendentals=0
        ),
        compiler_params=PARAMS,
        name="local",
    )(u, dep, masked, acc)
    out = pl.pallas_call(
        arrive_kernel,
        out_shape=shape((rows, cells), F32),
        in_specs=[VMEM] * (1 + blocks),
        out_specs=VMEM,
        compiler_params=PARAMS,
        name="arrive",
    )(local, *received)
    return out.reshape(fields, levels, cells)


def solution(mesh):
    return jax.shard_map(
        body,
        mesh=mesh,
        in_specs=(
            P(None, "lev", ("panel", "tile")),
            P(None, ("panel", "tile", "lev")),
            P(None, ("panel", "tile")),
            P(None, ("panel", "tile")),
            P(None, ("panel", "tile")),
            P(None, ("panel", "tile")),
        ),
        out_specs=P(None, "lev", ("panel", "tile")),
        check_vma=False,
    )
```

```python
import jax
import jax.numpy as jnp
from jax import lax
from jax.experimental import pallas as pl
from jax.experimental.pallas import tpu as pltpu
from jax.sharding import PartitionSpec as P

F32, BF16, I32 = jnp.float32, jnp.bfloat16, jnp.int32
LO = 256
LANES = 128
SUB = 8
VMEM = pl.BlockSpec(memory_space=pltpu.VMEM)
HBM = pl.BlockSpec(memory_space=pltpu.HBM)
PARAMS = pltpu.CompilerParams(vmem_limit_bytes=32 << 20)
NT = (((1,), (1,)), ((), ()))


def one_hot(rows, index):
    row = lax.broadcasted_iota(I32, (rows, index.shape[1]), 0)
    return (row == index).astype(F32).astype(BF16)


def two_terms(value):
    high = value.astype(BF16).astype(F32)
    return jnp.concatenate([high, value - high], axis=0)


def scatter_product(segments, cells):
    left = [[] for _ in range(cells // LO)]
    right = []
    for terms, target in segments:
        high = target // LO
        for h, row in enumerate(left):
            row.append(terms * (high == h).astype(F32).astype(BF16))
        right.append(one_hot(LO, target - high * LO))
    left = jnp.concatenate([jnp.concatenate(row, axis=1) for row in left], axis=0)
    return lax.dot_general(left, jnp.concatenate(right, axis=1), NT, preferred_element_type=F32)


def piece(steps, width):
    count = lax.axis_size("lev")
    source = lax.rem(lax.axis_index("lev") + (count - steps), count)
    return pl.ds(pl.multiple_of(source * width, LANES), width)


def scattered(u_ref, dep_ref, weight, k, at):
    return two_terms(u_ref[:, at] * weight).astype(BF16), dep_ref[k : k + 1, at]


def prepare_kernel(
    levels, early, u_hbm, w_hbm, dep_hbm, sp_hbm, bc_hbm, rot_hbm,
    u_ref, w_ref, dep_ref, keep_ref, picked_ref, lane_ref, tile_ref, live_ref, acc_ref,
    sp_ref, bc_ref, rot_ref, sems,
):
    pairs = [(sp_hbm, sp_ref), (bc_hbm, bc_ref), (rot_hbm, rot_ref), (dep_hbm, dep_ref), (u_hbm, u_ref), (w_hbm, w_ref)]
    copies = [pltpu.make_async_copy(a, b, sems.at[i]) for i, (a, b) in enumerate(pairs)]
    for c in copies:
        c.start()
    for c in copies[:3]:
        c.wait()
    rows, cells = u_ref.shape
    stencil = dep_ref.shape[0]
    blocks, slots = sp_ref.shape
    tiles = cells // LANES
    slot = lax.broadcasted_iota(I32, (1, slots), 1)
    which, columns, codes, lanes = [], [], [], []
    for j in range(blocks):
        chosen = sp_ref[j : j + 1, :]
        k = chosen // cells
        column = chosen - k * cells
        tile = column // LANES
        which.append(k)
        columns.append(column)
        alive = slot < bc_ref[0:1, j : j + 1]
        codes.append(jnp.where(alive, tile * SUB + k, -1))
        lanes.append(column - tile * LANES)
        lane_ref[j : j + 1, :] = lanes[j]
        tile_ref[j : j + 1, :] = tile
        live_ref[j : j + 1, :] = jnp.where(alive, k, -1)
    live = one_hot(tiles * SUB, jnp.concatenate(codes, axis=1))
    lane = one_hot(LANES, jnp.concatenate(lanes, axis=1))
    sent = lax.dot_general(live, lane, NT, preferred_element_type=F32)
    for t in range(tiles):
        keep_ref[:, t * LANES : (t + 1) * LANES] = 1.0 - sent[t * SUB : t * SUB + stencil]
    for c in copies[3:]:
        c.wait()
    dep = dep_ref[...]
    dep_high = dep // SUB
    dep_low = dep - dep_high * SUB
    table = jnp.concatenate(
        [two_terms(u_ref[...]), dep_high.astype(F32), dep_low.astype(F32), jnp.zeros((SUB, cells), F32)],
        axis=0,
    ).astype(BF16)
    column = jnp.concatenate(columns, axis=1)
    chunk = column // LO
    height = table.shape[0]
    got = jnp.dot(
        jnp.concatenate([table[:, c * LO : (c + 1) * LO] for c in range(cells // LO)], axis=0),
        one_hot(LO, column - chunk * LO),
        preferred_element_type=F32,
    )
    values = jnp.zeros((rows, blocks * slots), F32)
    targets = jnp.zeros((2 * stencil, blocks * slots), F32)
    for c in range(cells // LO):
        at = c * height
        here = chunk == c
        values = values + jnp.where(here, got[at : at + rows] + got[at + rows : at + 2 * rows], 0.0)
        targets = targets + jnp.where(here, got[at + 2 * rows : at + 2 * rows + 2 * stencil], 0.0)
    k = jnp.concatenate(which, axis=1)
    ids = jnp.zeros((1, blocks * slots), F32)
    for i in range(stencil):
        ids = ids + jnp.where(k == i, targets[i : i + 1] * SUB + targets[stencil + i : stencil + i + 1], 0.0)
    picked_ref[rows:, :] = jnp.broadcast_to(ids, (SUB, blocks * slots))
    picked_ref[2 * levels : rows, :] = values[2 * levels :]
    for j in range(blocks):
        here = slice(j * slots, (j + 1) * slots)
        zonal, merid = values[:levels, here], values[levels : 2 * levels, here]
        if j >= 2:
            code = rot_ref[0:1, j - 2 : j - 1]
            cosine = (code == 0).astype(F32) - (code == 2).astype(F32)
            sine = (code == 1).astype(F32) - (code == 3).astype(F32)
            zonal, merid = cosine * zonal + sine * merid, cosine * merid - sine * zonal
        picked_ref[:levels, here] = zonal
        picked_ref[levels : 2 * levels, here] = merid
    own = piece(0, w_ref.shape[1])
    acc_ref[...] = scatter_product(
        [scattered(u_ref, dep_ref, w_ref[k : k + 1, :] * keep_ref[k : k + 1, own], k, own) for k in range(early)], cells
    )


def send_kernel(count, paired, picked_ref, lane_ref, tile_ref, live_ref, *refs):
    parts, outs, full = refs[:count], refs[count:-1], refs[-1]
    stencil, cells = full.shape
    rows = picked_ref.shape[0] - SUB
    blocks, slots = lane_ref.shape
    for steps, part in enumerate(parts):
        full[:, piece(steps, part.shape[1])] = part[...]
    pad = jnp.zeros((SUB - stencil, LANES), F32)
    table = [
        jnp.concatenate([full[:, t * LANES : (t + 1) * LANES], pad], axis=0) for t in range(cells // LANES)
    ]
    row = lax.broadcasted_iota(I32, (SUB, slots), 0)
    message = []
    for j in range(blocks):
        lane = jnp.broadcast_to(lane_ref[j : j + 1, :], (SUB, slots))
        tile = jnp.broadcast_to(tile_ref[j : j + 1, :], (SUB, slots))
        found = jnp.zeros((SUB, slots), F32)
        for t, piece_t in enumerate(table):
            found = jnp.where(tile == t, jnp.take_along_axis(piece_t, lane, axis=1, mode="promise_in_bounds"), found)
        weight = jnp.sum(jnp.where(row == live_ref[j : j + 1, :], found, 0.0), axis=0, keepdims=True)
        here = slice(j * slots, (j + 1) * slots)
        message.append(jnp.concatenate([picked_ref[:rows, here] * weight, picked_ref[rows:, here]], axis=0))
    low, high, previous, following = message
    if paired:
        even = lax.rem(lax.axis_index("panel"), 2) == 0
        low, high = jnp.where(even, low, high), jnp.where(even, high, low)
    for out, m in zip(outs, [low, following, high, previous]):
        out[...] = m


def local_kernel(early, count, u_ref, dep_ref, w_ref, keep_ref, early_ref, acc_ref):
    stencil, cells = dep_ref.shape
    at = [(k, piece(s, cells // count)) for k in range(early) for s in range(1, count)]
    at += [(k, slice(None)) for k in range(early, stencil)]
    acc_ref[...] = early_ref[...] + scatter_product(
        [scattered(u_ref, dep_ref, w_ref[k : k + 1, here] * keep_ref[k : k + 1, here], k, here) for k, here in at], cells
    )


def arrive_kernel(acc_ref, *refs):
    received, out_ref = refs[:-1], refs[-1]
    rows, cells = out_ref.shape
    values = jnp.concatenate([r[:rows, :] for r in received], axis=1)
    ids = jnp.concatenate([r[rows : rows + 1, :] for r in received], axis=1).astype(I32)
    sums = scatter_product([(two_terms(values).astype(BF16), ids)], cells)
    for h in range(cells // LO):
        a, b, c = (2 * h * rows + i * rows for i in range(3))
        out_ref[:, h * LO : (h + 1) * LO] = (acc_ref[a:b] + acc_ref[b:c]) + (sums[a:b] + sums[b:c])


def rotated(value, axis, steps):
    count = lax.axis_size(axis)
    return lax.ppermute(value, axis, [(i, (i + steps) % count) for i in range(count)])


def racetrack(value, reverse):
    sectors, tiles = lax.axis_size("panel"), lax.axis_size("tile")
    route = []
    for p in range(sectors):
        step = 1 if (p % 2 == 0) != reverse else -1
        for t in range(tiles):
            q, to = (p, t + step) if 0 <= t + step < tiles else (p ^ 1, t)
            route.append((p * tiles + t, q * tiles + to))
    return lax.ppermute(value, ("panel", "tile"), route)


def body(adjoint_new, weights, departure, send_point, block_count, rotation):
    fields, levels, cells = adjoint_new.shape
    blocks, slots = send_point.shape
    stencil = departure.shape[0]
    rows = fields * levels
    count = lax.axis_size("lev")
    paired = lax.axis_size("panel") % 2 == 0
    points = blocks * slots
    early = 1
    shape = jax.ShapeDtypeStruct
    parts = [rotated(weights, "lev", s) for s in range(1, count)]
    inputs = (
        adjoint_new.reshape(rows, cells), weights, departure, send_point,
        block_count.reshape(1, -1), rotation.reshape(1, -1),
    )
    sums = shape((cells // LO * 2 * rows, LO), F32)
    u, own, dep, keep, picked, *slot_rows, acc = pl.pallas_call(
        lambda *refs: prepare_kernel(levels, early, *refs),
        out_shape=[
            shape((rows, cells), F32),
            shape(weights.shape, F32),
            shape((stencil, cells), I32),
            shape((stencil, cells), F32),
            shape((rows + SUB, points), F32),
            *([shape((blocks, slots), I32)] * 3),
            sums,
        ],
        in_specs=[HBM] * 6,
        out_specs=[VMEM] * 9,
        scratch_shapes=[
            pltpu.VMEM((blocks, slots), I32),
            pltpu.VMEM((1, block_count.size), I32),
            pltpu.VMEM((1, rotation.size), I32),
            pltpu.SemaphoreType.DMA((6,)),
        ],
        cost_estimate=pl.CostEstimate(
            flops=4 * rows * cells * points, bytes_accessed=8 * rows * cells, transcendentals=0
        ),
        compiler_params=PARAMS,
        name="prepare",
    )(*(pltpu.with_memory_space_constraint(a, pltpu.HBM) for a in inputs))
    block = shape((rows + SUB, slots), F32)
    *outgoing, full = pl.pallas_call(
        lambda *refs: send_kernel(count, paired, *refs),
        out_shape=[block] * blocks + [shape((stencil, cells), F32)],
        in_specs=[VMEM] * (4 + count),
        out_specs=[VMEM] * (blocks + 1),
        compiler_params=PARAMS,
        name="send",
    )(picked, *slot_rows, own, *parts)
    if paired:
        back, forth = (lambda v: racetrack(v, True)), (lambda v: racetrack(v, False))
    else:
        back, forth = (lambda v: rotated(v, "tile", -1)), (lambda v: rotated(v, "tile", 1))
    received = [
        back(outgoing[0]),
        rotated(outgoing[1], "panel", 1),
        forth(outgoing[2]),
        rotated(outgoing[3], "panel", -1),
    ]
    local = pl.pallas_call(
        lambda *refs: local_kernel(early, count, *refs),
        out_shape=sums,
        in_specs=[VMEM] * 5,
        out_specs=VMEM,
        cost_estimate=pl.CostEstimate(
            flops=4 * rows * cells * stencil * cells, bytes_accessed=8 * rows * cells, transcendentals=0
        ),
        compiler_params=PARAMS,
        name="local",
    )(u, dep, full, keep, acc)
    out = pl.pallas_call(
        arrive_kernel,
        out_shape=shape((rows, cells), F32),
        in_specs=[VMEM] * (1 + blocks),
        out_specs=VMEM,
        compiler_params=PARAMS,
        name="arrive",
    )(local, *received)
    return out.reshape(fields, levels, cells)


def solution(mesh):
    return jax.shard_map(
        body,
        mesh=mesh,
        in_specs=(
            P(None, "lev", ("panel", "tile")),
            P(None, ("panel", "tile", "lev")),
            P(None, ("panel", "tile")),
            P(None, ("panel", "tile")),
            P(None, ("panel", "tile")),
            P(None, ("panel", "tile")),
        ),
        out_specs=P(None, "lev", ("panel", "tile")),
        check_vma=False,
    )
```

```python
import jax
import jax.numpy as jnp
from jax import lax
from jax.experimental import pallas as pl
from jax.experimental.pallas import tpu as pltpu
from jax.sharding import PartitionSpec as P

F32, BF16, I32 = jnp.float32, jnp.bfloat16, jnp.int32
LO = 256
LANES = 128
SUB = 8
VMEM = pl.BlockSpec(memory_space=pltpu.VMEM)
HBM = pl.BlockSpec(memory_space=pltpu.HBM)
PARAMS = pltpu.CompilerParams(vmem_limit_bytes=32 << 20)
NT = (((1,), (1,)), ((), ()))


def one_hot(rows, index):
    row = lax.broadcasted_iota(I32, (rows, index.shape[1]), 0)
    return (row == index).astype(F32).astype(BF16)


def two_terms(value):
    high = value.astype(BF16).astype(F32)
    return jnp.concatenate([high, value - high], axis=0)


def scatter_product(segments, cells):
    left = [[] for _ in range(cells // LO)]
    right = []
    for terms, target in segments:
        high = target // LO
        for h, row in enumerate(left):
            row.append(terms * (high == h).astype(F32).astype(BF16))
        right.append(one_hot(LO, target - high * LO))
    left = jnp.concatenate([jnp.concatenate(row, axis=1) for row in left], axis=0)
    return lax.dot_general(left, jnp.concatenate(right, axis=1), NT, preferred_element_type=F32)


def piece(steps, width):
    count = lax.axis_size("lev")
    source = lax.rem(lax.axis_index("lev") + (count - steps), count)
    return pl.ds(pl.multiple_of(source * width, LANES), width)


def scattered(u_ref, dep_ref, weight, k, at):
    return two_terms(u_ref[:, at] * weight).astype(BF16), dep_ref[k : k + 1, at]


def picked_lanes(tiles, lane, tile):
    found = jnp.zeros(lane.shape, F32)
    for t, table in enumerate(tiles):
        found = jnp.where(tile == t, jnp.take_along_axis(table, lane, axis=1, mode="promise_in_bounds"), found)
    return found


def prepare_kernel(
    levels, early, u_hbm, w_hbm, dep_hbm, sp_hbm, bc_hbm, rot_hbm,
    u_ref, w_ref, dep_ref, keep_ref, picked_ref, lane_ref, tile_ref, live_ref, acc_ref,
    sp_ref, bc_ref, rot_ref, sems,
):
    pairs = [(sp_hbm, sp_ref), (bc_hbm, bc_ref), (rot_hbm, rot_ref), (dep_hbm, dep_ref), (u_hbm, u_ref), (w_hbm, w_ref)]
    copies = [pltpu.make_async_copy(a, b, sems.at[i]) for i, (a, b) in enumerate(pairs)]
    for c in copies:
        c.start()
    for c in copies[:3]:
        c.wait()
    rows, cells = u_ref.shape
    stencil = dep_ref.shape[0]
    blocks, slots = sp_ref.shape
    tiles = cells // LANES
    slot = lax.broadcasted_iota(I32, (1, slots), 1)
    which, codes, lanes = [], [], []
    for j in range(blocks):
        chosen = sp_ref[j : j + 1, :]
        k = chosen // cells
        column = chosen - k * cells
        tile = column // LANES
        which.append(k)
        alive = slot < bc_ref[0:1, j : j + 1]
        codes.append(jnp.where(alive, tile * SUB + k, -1))
        lanes.append(column - tile * LANES)
        lane_ref[j : j + 1, :] = lanes[j]
        tile_ref[j : j + 1, :] = tile
        live_ref[j : j + 1, :] = jnp.where(alive, k, -1)
    live = one_hot(tiles * SUB, jnp.concatenate(codes, axis=1))
    lane = one_hot(LANES, jnp.concatenate(lanes, axis=1))
    sent = lax.dot_general(live, lane, NT, preferred_element_type=F32)
    for t in range(tiles):
        keep_ref[:, t * LANES : (t + 1) * LANES] = 1.0 - sent[t * SUB : t * SUB + stencil]
    for c in copies[3:]:
        c.wait()
    pad = jnp.zeros((SUB - stencil, LANES), F32)
    spans = [slice(t * LANES, (t + 1) * LANES) for t in range(tiles)]
    targets = [jnp.concatenate([dep_ref[:, span].astype(F32), pad], axis=0) for span in spans]
    row = lax.broadcasted_iota(I32, (SUB, slots), 0)
    for j in range(blocks):
        here = slice(j * slots, (j + 1) * slots)
        at = jnp.broadcast_to(lane_ref[j : j + 1, :], (SUB, slots)), jnp.broadcast_to(tile_ref[j : j + 1, :], (SUB, slots))
        ids = jnp.where(row == which[j], picked_lanes(targets, *at), 0.0)
        picked_ref[rows:, here] = jnp.broadcast_to(jnp.sum(ids, axis=0, keepdims=True), (SUB, slots))
        values = jnp.concatenate(
            [picked_lanes([u_ref[g : g + SUB, span] for span in spans], *at) for g in range(0, rows, SUB)], axis=0
        )
        zonal, merid = values[:levels], values[levels : 2 * levels]
        if j >= 2:
            code = rot_ref[0:1, j - 2 : j - 1]
            cosine = (code == 0).astype(F32) - (code == 2).astype(F32)
            sine = (code == 1).astype(F32) - (code == 3).astype(F32)
            zonal, merid = cosine * zonal + sine * merid, cosine * merid - sine * zonal
        picked_ref[:levels, here] = zonal
        picked_ref[levels : 2 * levels, here] = merid
        picked_ref[2 * levels : rows, here] = values[2 * levels :]
    own = piece(0, w_ref.shape[1])
    acc_ref[...] = scatter_product(
        [scattered(u_ref, dep_ref, w_ref[k : k + 1, :] * keep_ref[k : k + 1, own], k, own) for k in range(early)], cells
    )


def send_kernel(count, paired, picked_ref, lane_ref, tile_ref, live_ref, *refs):
    parts, outs, full = refs[:count], refs[count:-1], refs[-1]
    stencil, cells = full.shape
    rows = picked_ref.shape[0] - SUB
    blocks, slots = lane_ref.shape
    for steps, part in enumerate(parts):
        full[:, piece(steps, part.shape[1])] = part[...]
    pad = jnp.zeros((SUB - stencil, LANES), F32)
    table = [
        jnp.concatenate([full[:, t * LANES : (t + 1) * LANES], pad], axis=0) for t in range(cells // LANES)
    ]
    row = lax.broadcasted_iota(I32, (SUB, slots), 0)
    message = []
    for j in range(blocks):
        lane = jnp.broadcast_to(lane_ref[j : j + 1, :], (SUB, slots))
        tile = jnp.broadcast_to(tile_ref[j : j + 1, :], (SUB, slots))
        found = picked_lanes(table, lane, tile)
        weight = jnp.sum(jnp.where(row == live_ref[j : j + 1, :], found, 0.0), axis=0, keepdims=True)
        here = slice(j * slots, (j + 1) * slots)
        message.append(jnp.concatenate([picked_ref[:rows, here] * weight, picked_ref[rows:, here]], axis=0))
    low, high, previous, following = message
    if paired:
        even = lax.rem(lax.axis_index("panel"), 2) == 0
        low, high = jnp.where(even, low, high), jnp.where(even, high, low)
    for out, m in zip(outs, [low, following, high, previous]):
        out[...] = m


def local_kernel(early, count, u_ref, dep_ref, w_ref, keep_ref, early_ref, acc_ref):
    stencil, cells = dep_ref.shape
    at = [(k, piece(s, cells // count)) for k in range(early) for s in range(1, count)]
    at += [(k, slice(None)) for k in range(early, stencil)]
    acc_ref[...] = early_ref[...] + scatter_product(
        [scattered(u_ref, dep_ref, w_ref[k : k + 1, here] * keep_ref[k : k + 1, here], k, here) for k, here in at], cells
    )


def arrived_sums(received, cells):
    rows = received[0].shape[0] - SUB
    values = jnp.concatenate([r[:rows, :] for r in received], axis=1)
    ids = jnp.concatenate([r[rows : rows + 1, :] for r in received], axis=1).astype(I32)
    sums = scatter_product([(two_terms(values).astype(BF16), ids)], cells)
    return [
        sums[2 * h * rows : (2 * h + 1) * rows] + sums[(2 * h + 1) * rows : (2 * h + 2) * rows]
        for h in range(cells // LO)
    ]


def merge_kernel(acc_ref, *refs):
    received, out_ref = refs[:-1], refs[-1]
    rows, cells = out_ref.shape
    for h, sums in enumerate(arrived_sums(received, cells)):
        a, b, c = (2 * h * rows + i * rows for i in range(3))
        out_ref[:, h * LO : (h + 1) * LO] = (acc_ref[a:b] + acc_ref[b:c]) + sums


def arrive_kernel(merged_ref, *refs):
    received, out_ref = refs[:-1], refs[-1]
    for h, sums in enumerate(arrived_sums(received, out_ref.shape[1])):
        here = slice(h * LO, (h + 1) * LO)
        out_ref[:, here] = merged_ref[:, here] + sums


def rotated(value, axis, steps):
    count = lax.axis_size(axis)
    return lax.ppermute(value, axis, [(i, (i + steps) % count) for i in range(count)])


def racetrack(value, reverse):
    sectors, tiles = lax.axis_size("panel"), lax.axis_size("tile")
    route = []
    for p in range(sectors):
        step = 1 if (p % 2 == 0) != reverse else -1
        for t in range(tiles):
            q, to = (p, t + step) if 0 <= t + step < tiles else (p ^ 1, t)
            route.append((p * tiles + t, q * tiles + to))
    return lax.ppermute(value, ("panel", "tile"), route)


def body(adjoint_new, weights, departure, send_point, block_count, rotation):
    fields, levels, cells = adjoint_new.shape
    blocks, slots = send_point.shape
    stencil = departure.shape[0]
    rows = fields * levels
    count = lax.axis_size("lev")
    paired = lax.axis_size("panel") % 2 == 0
    points = blocks * slots
    early = 1
    shape = jax.ShapeDtypeStruct
    parts = [rotated(weights, "lev", s) for s in range(1, count)]
    inputs = (
        adjoint_new.reshape(rows, cells), weights, departure, send_point,
        block_count.reshape(1, -1), rotation.reshape(1, -1),
    )
    sums = shape((cells // LO * 2 * rows, LO), F32)
    u, own, dep, keep, picked, *slot_rows, acc = pl.pallas_call(
        lambda *refs: prepare_kernel(levels, early, *refs),
        out_shape=[
            shape((rows, cells), F32),
            shape(weights.shape, F32),
            shape((stencil, cells), I32),
            shape((stencil, cells), F32),
            shape((rows + SUB, points), F32),
            *([shape((blocks, slots), I32)] * 3),
            sums,
        ],
        in_specs=[HBM] * 6,
        out_specs=[VMEM] * 9,
        scratch_shapes=[
            pltpu.VMEM((blocks, slots), I32),
            pltpu.VMEM((1, block_count.size), I32),
            pltpu.VMEM((1, rotation.size), I32),
            pltpu.SemaphoreType.DMA((6,)),
        ],
        cost_estimate=pl.CostEstimate(
            flops=4 * rows * cells * points, bytes_accessed=8 * rows * cells, transcendentals=0
        ),
        compiler_params=PARAMS,
        name="prepare",
    )(*(pltpu.with_memory_space_constraint(a, pltpu.HBM) for a in inputs))
    block = shape((rows + SUB, slots), F32)
    *outgoing, full = pl.pallas_call(
        lambda *refs: send_kernel(count, paired, *refs),
        out_shape=[block] * blocks + [shape((stencil, cells), F32)],
        in_specs=[VMEM] * (4 + count),
        out_specs=[VMEM] * (blocks + 1),
        compiler_params=PARAMS,
        name="send",
    )(picked, *slot_rows, own, *parts)
    if paired:
        back, forth = (lambda v: racetrack(v, True)), (lambda v: racetrack(v, False))
    else:
        back, forth = (lambda v: rotated(v, "tile", -1)), (lambda v: rotated(v, "tile", 1))
    received = [
        back(outgoing[0]),
        rotated(outgoing[1], "panel", 1),
        forth(outgoing[2]),
        rotated(outgoing[3], "panel", -1),
    ]
    acc = pl.pallas_call(
        lambda *refs: local_kernel(early, count, *refs),
        out_shape=sums,
        in_specs=[VMEM] * 5,
        out_specs=VMEM,
        cost_estimate=pl.CostEstimate(
            flops=4 * rows * cells * stencil * cells, bytes_accessed=8 * rows * cells, transcendentals=0
        ),
        compiler_params=PARAMS,
        name="local",
    )(u, dep, full, keep, acc)
    result = shape((rows, cells), F32)
    merged = pl.pallas_call(
        merge_kernel,
        out_shape=result,
        in_specs=[VMEM] * blocks,
        out_specs=VMEM,
        cost_estimate=pl.CostEstimate(
            flops=4 * rows * cells * points, bytes_accessed=8 * rows * cells, transcendentals=0
        ),
        compiler_params=PARAMS,
        name="merge",
    )(acc, *received[:-1])
    out = pl.pallas_call(
        arrive_kernel,
        out_shape=result,
        in_specs=[VMEM] * 2,
        out_specs=VMEM,
        compiler_params=PARAMS,
        name="arrive",
    )(merged, received[-1])
    return out.reshape(fields, levels, cells)


def solution(mesh):
    return jax.shard_map(
        body,
        mesh=mesh,
        in_specs=(
            P(None, "lev", ("panel", "tile")),
            P(None, ("panel", "tile", "lev")),
            P(None, ("panel", "tile")),
            P(None, ("panel", "tile")),
            P(None, ("panel", "tile")),
            P(None, ("panel", "tile")),
        ),
        out_specs=P(None, "lev", ("panel", "tile")),
        check_vma=False,
    )
```

```python
import jax
import jax.numpy as jnp
from jax import lax
from jax.experimental import pallas as pl
from jax.experimental.pallas import tpu as pltpu
from jax.sharding import PartitionSpec as P

F32, BF16, I32 = jnp.float32, jnp.bfloat16, jnp.int32
LO = 256
LANES = 128
SUB = 8
VMEM = pl.BlockSpec(memory_space=pltpu.VMEM)
HBM = pl.BlockSpec(memory_space=pltpu.HBM)
PARAMS = pltpu.CompilerParams(vmem_limit_bytes=32 << 20)
NT = (((1,), (1,)), ((), ()))


def one_hot(rows, index):
    row = lax.broadcasted_iota(I32, (rows, index.shape[1]), 0)
    return (row == index).astype(F32).astype(BF16)


def two_terms(value):
    high = value.astype(BF16).astype(F32)
    return jnp.concatenate([high, value - high], axis=0)


def scatter_product(segments, cells):
    left = [[] for _ in range(cells // LO)]
    right = []
    for terms, target in segments:
        high = target // LO
        for h, row in enumerate(left):
            row.append(terms * (high == h).astype(F32).astype(BF16))
        right.append(one_hot(LO, target - high * LO))
    left = jnp.concatenate([jnp.concatenate(row, axis=1) for row in left], axis=0)
    return lax.dot_general(left, jnp.concatenate(right, axis=1), NT, preferred_element_type=F32)


def piece(steps, width):
    count = lax.axis_size("lev")
    source = lax.rem(lax.axis_index("lev") + (count - steps), count)
    return pl.ds(pl.multiple_of(source * width, LANES), width)


def scattered(u_ref, dep_ref, weight, k, at):
    return two_terms(u_ref[:, at] * weight).astype(BF16), dep_ref[k : k + 1, at]


def picked_lanes(tiles, lane, tile):
    found = jnp.zeros(lane.shape, F32)
    for t, table in enumerate(tiles):
        found = jnp.where(tile == t, jnp.take_along_axis(table, lane, axis=1, mode="promise_in_bounds"), found)
    return found


def prepare_kernel(
    levels, early, u_hbm, w_hbm, dep_hbm, sp_hbm, bc_hbm, rot_hbm,
    u_ref, w_ref, dep_ref, keep_ref, picked_ref, lane_ref, tile_ref, live_ref, acc_ref,
    sp_ref, bc_ref, rot_ref, sems,
):
    pairs = [(sp_hbm, sp_ref), (bc_hbm, bc_ref), (rot_hbm, rot_ref), (dep_hbm, dep_ref), (u_hbm, u_ref), (w_hbm, w_ref)]
    copies = [pltpu.make_async_copy(a, b, sems.at[i]) for i, (a, b) in enumerate(pairs)]
    for c in copies:
        c.start()
    for c in copies[:3]:
        c.wait()
    rows, cells = u_ref.shape
    stencil = dep_ref.shape[0]
    blocks, slots = sp_ref.shape
    tiles = cells // LANES
    slot = lax.broadcasted_iota(I32, (1, slots), 1)
    which, codes, lanes = [], [], []
    for j in range(blocks):
        chosen = sp_ref[j : j + 1, :]
        k = chosen // cells
        column = chosen - k * cells
        tile = column // LANES
        which.append(k)
        alive = slot < bc_ref[0:1, j : j + 1]
        codes.append(jnp.where(alive, tile * SUB + k, -1))
        lanes.append(column - tile * LANES)
        lane_ref[j : j + 1, :] = lanes[j]
        tile_ref[j : j + 1, :] = tile
        live_ref[j : j + 1, :] = jnp.where(alive, k, -1)
    live = one_hot(tiles * SUB, jnp.concatenate(codes, axis=1))
    lane = one_hot(LANES, jnp.concatenate(lanes, axis=1))
    sent = lax.dot_general(live, lane, NT, preferred_element_type=F32)
    for t in range(tiles):
        keep_ref[:, t * LANES : (t + 1) * LANES] = 1.0 - sent[t * SUB : t * SUB + stencil]
    for c in copies[3:]:
        c.wait()
    pad = jnp.zeros((SUB - stencil, LANES), F32)
    spans = [slice(t * LANES, (t + 1) * LANES) for t in range(tiles)]
    targets = [jnp.concatenate([dep_ref[:, span].astype(F32), pad], axis=0) for span in spans]
    row = lax.broadcasted_iota(I32, (SUB, slots), 0)
    for j in range(blocks):
        here = slice(j * slots, (j + 1) * slots)
        at = jnp.broadcast_to(lane_ref[j : j + 1, :], (SUB, slots)), jnp.broadcast_to(tile_ref[j : j + 1, :], (SUB, slots))
        ids = jnp.where(row == which[j], picked_lanes(targets, *at), 0.0)
        picked_ref[rows:, here] = jnp.broadcast_to(jnp.sum(ids, axis=0, keepdims=True), (SUB, slots))
        values = jnp.concatenate(
            [picked_lanes([u_ref[g : g + SUB, span] for span in spans], *at) for g in range(0, rows, SUB)], axis=0
        )
        zonal, merid = values[:levels], values[levels : 2 * levels]
        if j >= 2:
            code = rot_ref[0:1, j - 2 : j - 1]
            cosine = (code == 0).astype(F32) - (code == 2).astype(F32)
            sine = (code == 1).astype(F32) - (code == 3).astype(F32)
            zonal, merid = cosine * zonal + sine * merid, cosine * merid - sine * zonal
        picked_ref[:levels, here] = zonal
        picked_ref[levels : 2 * levels, here] = merid
        picked_ref[2 * levels : rows, here] = values[2 * levels :]
    own = piece(0, w_ref.shape[1])
    acc_ref[...] = scatter_product(
        [scattered(u_ref, dep_ref, w_ref[k : k + 1, :] * keep_ref[k : k + 1, own], k, own) for k in range(early)], cells
    )


def send_kernel(count, paired, picked_ref, lane_ref, tile_ref, live_ref, *refs):
    parts, outs, full = refs[:count], refs[count:-1], refs[-1]
    stencil, cells = full.shape
    rows = picked_ref.shape[0] - SUB
    blocks, slots = lane_ref.shape
    for steps, part in enumerate(parts):
        full[:, piece(steps, part.shape[1])] = part[...]
    pad = jnp.zeros((SUB - stencil, LANES), F32)
    table = [
        jnp.concatenate([full[:, t * LANES : (t + 1) * LANES], pad], axis=0) for t in range(cells // LANES)
    ]
    row = lax.broadcasted_iota(I32, (SUB, slots), 0)
    message = []
    for j in range(blocks):
        lane = jnp.broadcast_to(lane_ref[j : j + 1, :], (SUB, slots))
        tile = jnp.broadcast_to(tile_ref[j : j + 1, :], (SUB, slots))
        found = picked_lanes(table, lane, tile)
        weight = jnp.sum(jnp.where(row == live_ref[j : j + 1, :], found, 0.0), axis=0, keepdims=True)
        here = slice(j * slots, (j + 1) * slots)
        message.append(jnp.concatenate([picked_ref[:rows, here] * weight, picked_ref[rows:, here]], axis=0))
    low, high, previous, following = message
    if paired:
        even = lax.rem(lax.axis_index("panel"), 2) == 0
        low, high = jnp.where(even, low, high), jnp.where(even, high, low)
    for out, m in zip(outs, [low, following, high, previous]):
        out[...] = m


def local_kernel(early, count, u_ref, dep_ref, w_ref, keep_ref, early_ref, acc_ref):
    stencil, cells = dep_ref.shape
    at = [(k, piece(s, cells // count)) for k in range(early) for s in range(1, count)]
    at += [(k, slice(None)) for k in range(early, stencil)]
    acc_ref[...] = early_ref[...] + scatter_product(
        [scattered(u_ref, dep_ref, w_ref[k : k + 1, here] * keep_ref[k : k + 1, here], k, here) for k, here in at], cells
    )


def arrive_kernel(acc_ref, *refs):
    received, out_ref = refs[:-1], refs[-1]
    rows, cells = out_ref.shape
    values = jnp.concatenate([r[:rows, :] for r in received], axis=1)
    ids = jnp.concatenate([r[rows : rows + 1, :] for r in received], axis=1).astype(I32)
    sums = scatter_product([(two_terms(values).astype(BF16), ids)], cells)
    for h in range(cells // LO):
        a, b, c = (2 * h * rows + i * rows for i in range(3))
        out_ref[:, h * LO : (h + 1) * LO] = (acc_ref[a:b] + acc_ref[b:c]) + (sums[a:b] + sums[b:c])


def rotated(value, axis, steps):
    count = lax.axis_size(axis)
    return lax.ppermute(value, axis, [(i, (i + steps) % count) for i in range(count)])


def racetrack(value, reverse):
    sectors, tiles = lax.axis_size("panel"), lax.axis_size("tile")
    route = []
    for p in range(sectors):
        step = 1 if (p % 2 == 0) != reverse else -1
        for t in range(tiles):
            q, to = (p, t + step) if 0 <= t + step < tiles else (p ^ 1, t)
            route.append((p * tiles + t, q * tiles + to))
    return lax.ppermute(value, ("panel", "tile"), route)


def body(adjoint_new, weights, departure, send_point, block_count, rotation):
    fields, levels, cells = adjoint_new.shape
    blocks, slots = send_point.shape
    stencil = departure.shape[0]
    rows = fields * levels
    count = lax.axis_size("lev")
    paired = lax.axis_size("panel") % 2 == 0
    points = blocks * slots
    early = 2
    shape = jax.ShapeDtypeStruct
    parts = [rotated(weights, "lev", s) for s in range(1, count)]
    inputs = (
        adjoint_new.reshape(rows, cells), weights, departure, send_point,
        block_count.reshape(1, -1), rotation.reshape(1, -1),
    )
    sums = shape((cells // LO * 2 * rows, LO), F32)
    u, own, dep, keep, picked, *slot_rows, acc = pl.pallas_call(
        lambda *refs: prepare_kernel(levels, early, *refs),
        out_shape=[
            shape((rows, cells), F32),
            shape(weights.shape, F32),
            shape((stencil, cells), I32),
            shape((stencil, cells), F32),
            shape((rows + SUB, points), F32),
            *([shape((blocks, slots), I32)] * 3),
            sums,
        ],
        in_specs=[HBM] * 6,
        out_specs=[VMEM] * 9,
        scratch_shapes=[
            pltpu.VMEM((blocks, slots), I32),
            pltpu.VMEM((1, block_count.size), I32),
            pltpu.VMEM((1, rotation.size), I32),
            pltpu.SemaphoreType.DMA((6,)),
        ],
        cost_estimate=pl.CostEstimate(
            flops=4 * rows * cells * points, bytes_accessed=8 * rows * cells, transcendentals=0
        ),
        compiler_params=PARAMS,
        name="prepare",
    )(*(pltpu.with_memory_space_constraint(a, pltpu.HBM) for a in inputs))
    block = shape((rows + SUB, slots), F32)
    *outgoing, full = pl.pallas_call(
        lambda *refs: send_kernel(count, paired, *refs),
        out_shape=[block] * blocks + [shape((stencil, cells), F32)],
        in_specs=[VMEM] * (4 + count),
        out_specs=[VMEM] * (blocks + 1),
        compiler_params=PARAMS,
        name="send",
    )(picked, *slot_rows, own, *parts)
    if paired:
        back, forth = (lambda v: racetrack(v, True)), (lambda v: racetrack(v, False))
    else:
        back, forth = (lambda v: rotated(v, "tile", -1)), (lambda v: rotated(v, "tile", 1))
    received = [
        back(outgoing[0]),
        rotated(outgoing[1], "panel", 1),
        forth(outgoing[2]),
        rotated(outgoing[3], "panel", -1),
    ]
    acc = pl.pallas_call(
        lambda *refs: local_kernel(early, count, *refs),
        out_shape=sums,
        in_specs=[VMEM] * 5,
        out_specs=VMEM,
        cost_estimate=pl.CostEstimate(
            flops=4 * rows * cells * stencil * cells, bytes_accessed=8 * rows * cells, transcendentals=0
        ),
        compiler_params=PARAMS,
        name="local",
    )(u, dep, full, keep, acc)
    out = pl.pallas_call(
        arrive_kernel,
        out_shape=shape((rows, cells), F32),
        in_specs=[VMEM] * (1 + blocks),
        out_specs=VMEM,
        compiler_params=PARAMS,
        name="arrive",
    )(acc, *received)
    return out.reshape(fields, levels, cells)


def solution(mesh):
    return jax.shard_map(
        body,
        mesh=mesh,
        in_specs=(
            P(None, "lev", ("panel", "tile")),
            P(None, ("panel", "tile", "lev")),
            P(None, ("panel", "tile")),
            P(None, ("panel", "tile")),
            P(None, ("panel", "tile")),
            P(None, ("panel", "tile")),
        ),
        out_specs=P(None, "lev", ("panel", "tile")),
        check_vma=False,
    )
```

```python
import jax
import jax.numpy as jnp
from jax import lax
from jax.experimental import pallas as pl
from jax.experimental.pallas import tpu as pltpu
from jax.sharding import PartitionSpec as P

F32, BF16, I32 = jnp.float32, jnp.bfloat16, jnp.int32
LO = 256
LANES = 128
SUB = 8
VMEM = pl.BlockSpec(memory_space=pltpu.VMEM)
HBM = pl.BlockSpec(memory_space=pltpu.HBM)
PARAMS = pltpu.CompilerParams(vmem_limit_bytes=32 << 20)
NT = (((1,), (1,)), ((), ()))


def one_hot(rows, index):
    row = lax.broadcasted_iota(I32, (rows, index.shape[1]), 0)
    return (row == index).astype(F32).astype(BF16)


def two_terms(value):
    high = value.astype(BF16).astype(F32)
    return jnp.concatenate([high, value - high], axis=0)


def scatter_product(segments, cells):
    left = [[] for _ in range(cells // LO)]
    right = []
    for terms, target in segments:
        high = target // LO
        for h, row in enumerate(left):
            row.append(terms * (high == h).astype(F32).astype(BF16))
        right.append(one_hot(LO, target - high * LO))
    left = jnp.concatenate([jnp.concatenate(row, axis=1) for row in left], axis=0)
    return lax.dot_general(left, jnp.concatenate(right, axis=1), NT, preferred_element_type=F32)


def piece(steps, width):
    count = lax.axis_size("lev")
    source = lax.rem(lax.axis_index("lev") + (count - steps), count)
    return pl.ds(pl.multiple_of(source * width, LANES), width)


def scattered(u_ref, dep_ref, weight, k, at):
    return two_terms(u_ref[:, at] * weight).astype(BF16), dep_ref[k : k + 1, at]


def picked_lanes(tiles, lane, tile):
    found = jnp.zeros(lane.shape, F32)
    for t, table in enumerate(tiles):
        found = jnp.where(tile == t, jnp.take_along_axis(table, lane, axis=1, mode="promise_in_bounds"), found)
    return found


def prepare_kernel(
    levels, early, u_hbm, w_hbm, dep_hbm, sp_hbm, bc_hbm, rot_hbm,
    u_ref, w_ref, dep_ref, keep_ref, picked_ref, lane_ref, tile_ref, live_ref, acc_ref,
    sp_ref, bc_ref, rot_ref, sems,
):
    pairs = [(sp_hbm, sp_ref), (bc_hbm, bc_ref), (rot_hbm, rot_ref), (dep_hbm, dep_ref), (u_hbm, u_ref), (w_hbm, w_ref)]
    copies = [pltpu.make_async_copy(a, b, sems.at[i]) for i, (a, b) in enumerate(pairs)]
    for c in copies:
        c.start()
    for c in copies[:3]:
        c.wait()
    rows, cells = u_ref.shape
    stencil = dep_ref.shape[0]
    blocks, slots = sp_ref.shape
    tiles = cells // LANES
    slot = lax.broadcasted_iota(I32, (1, slots), 1)
    which, codes, lanes = [], [], []
    for j in range(blocks):
        chosen = sp_ref[j : j + 1, :]
        k = chosen // cells
        column = chosen - k * cells
        tile = column // LANES
        which.append(k)
        alive = slot < bc_ref[0:1, j : j + 1]
        codes.append(jnp.where(alive, tile * SUB + k, -1))
        lanes.append(column - tile * LANES)
        lane_ref[j : j + 1, :] = lanes[j]
        tile_ref[j : j + 1, :] = tile
        live_ref[j : j + 1, :] = jnp.where(alive, k, -1)
    live = one_hot(tiles * SUB, jnp.concatenate(codes, axis=1))
    lane = one_hot(LANES, jnp.concatenate(lanes, axis=1))
    sent = lax.dot_general(live, lane, NT, preferred_element_type=F32)
    for t in range(tiles):
        keep_ref[:, t * LANES : (t + 1) * LANES] = 1.0 - sent[t * SUB : t * SUB + stencil]
    for c in copies[3:]:
        c.wait()
    pad = jnp.zeros((SUB - stencil, LANES), F32)
    spans = [slice(t * LANES, (t + 1) * LANES) for t in range(tiles)]
    targets = [jnp.concatenate([dep_ref[:, span].astype(F32), pad], axis=0) for span in spans]
    row = lax.broadcasted_iota(I32, (SUB, slots), 0)
    for j in range(blocks):
        here = slice(j * slots, (j + 1) * slots)
        at = jnp.broadcast_to(lane_ref[j : j + 1, :], (SUB, slots)), jnp.broadcast_to(tile_ref[j : j + 1, :], (SUB, slots))
        ids = jnp.where(row == which[j], picked_lanes(targets, *at), 0.0)
        picked_ref[rows:, here] = jnp.broadcast_to(jnp.sum(ids, axis=0, keepdims=True), (SUB, slots))
        values = jnp.concatenate(
            [picked_lanes([u_ref[g : g + SUB, span] for span in spans], *at) for g in range(0, rows, SUB)], axis=0
        )
        zonal, merid = values[:levels], values[levels : 2 * levels]
        if j >= 2:
            code = rot_ref[0:1, j - 2 : j - 1]
            cosine = (code == 0).astype(F32) - (code == 2).astype(F32)
            sine = (code == 1).astype(F32) - (code == 3).astype(F32)
            zonal, merid = cosine * zonal + sine * merid, cosine * merid - sine * zonal
        picked_ref[:levels, here] = zonal
        picked_ref[levels : 2 * levels, here] = merid
        picked_ref[2 * levels : rows, here] = values[2 * levels :]
    own = piece(0, w_ref.shape[1])
    acc_ref[...] = scatter_product(
        [scattered(u_ref, dep_ref, w_ref[k : k + 1, :] * keep_ref[k : k + 1, own], k, own) for k in range(early)], cells
    )


def send_kernel(count, paired, picked_ref, lane_ref, tile_ref, live_ref, *refs):
    parts, outs, full = refs[:count], refs[count:-1], refs[-1]
    stencil, cells = full.shape
    rows = picked_ref.shape[0] - SUB
    blocks, slots = lane_ref.shape
    for steps, part in enumerate(parts):
        full[:, piece(steps, part.shape[1])] = part[...]
    pad = jnp.zeros((SUB - stencil, LANES), F32)
    table = [
        jnp.concatenate([full[:, t * LANES : (t + 1) * LANES], pad], axis=0) for t in range(cells // LANES)
    ]
    row = lax.broadcasted_iota(I32, (SUB, slots), 0)
    message = []
    for j in range(blocks):
        lane = jnp.broadcast_to(lane_ref[j : j + 1, :], (SUB, slots))
        tile = jnp.broadcast_to(tile_ref[j : j + 1, :], (SUB, slots))
        found = picked_lanes(table, lane, tile)
        weight = jnp.sum(jnp.where(row == live_ref[j : j + 1, :], found, 0.0), axis=0, keepdims=True)
        here = slice(j * slots, (j + 1) * slots)
        message.append(jnp.concatenate([picked_ref[:rows, here] * weight, picked_ref[rows:, here]], axis=0))
    low, high, previous, following = message
    if paired:
        even = lax.rem(lax.axis_index("panel"), 2) == 0
        low, high = jnp.where(even, low, high), jnp.where(even, high, low)
    for out, m in zip(outs, [low, following, high, previous]):
        out[...] = m


def local_kernel(early, count, u_ref, dep_ref, w_ref, keep_ref, early_ref, acc_ref):
    stencil, cells = dep_ref.shape
    at = [(k, piece(s, cells // count)) for k in range(early) for s in range(1, count)]
    at += [(k, slice(None)) for k in range(early, stencil)]
    acc_ref[...] = early_ref[...] + scatter_product(
        [scattered(u_ref, dep_ref, w_ref[k : k + 1, here] * keep_ref[k : k + 1, here], k, here) for k, here in at], cells
    )


def arrived_sums(received, cells):
    rows = received[0].shape[0] - SUB
    values = jnp.concatenate([r[:rows, :] for r in received], axis=1)
    ids = jnp.concatenate([r[rows : rows + 1, :] for r in received], axis=1).astype(I32)
    sums = scatter_product([(two_terms(values).astype(BF16), ids)], cells)
    return [
        sums[2 * h * rows : (2 * h + 1) * rows] + sums[(2 * h + 1) * rows : (2 * h + 2) * rows]
        for h in range(cells // LO)
    ]


def merge_kernel(acc_ref, *refs):
    received, out_ref = refs[:-1], refs[-1]
    rows, cells = out_ref.shape
    for h, sums in enumerate(arrived_sums(received, cells)):
        a, b, c = (2 * h * rows + i * rows for i in range(3))
        out_ref[:, h * LO : (h + 1) * LO] = (acc_ref[a:b] + acc_ref[b:c]) + sums


def arrive_kernel(merged_ref, *refs):
    received, out_ref = refs[:-1], refs[-1]
    for h, sums in enumerate(arrived_sums(received, out_ref.shape[1])):
        here = slice(h * LO, (h + 1) * LO)
        out_ref[:, here] = merged_ref[:, here] + sums


def rotated(value, axis, steps):
    count = lax.axis_size(axis)
    return lax.ppermute(value, axis, [(i, (i + steps) % count) for i in range(count)])


def racetrack(value, reverse):
    sectors, tiles = lax.axis_size("panel"), lax.axis_size("tile")
    route = []
    for p in range(sectors):
        step = 1 if (p % 2 == 0) != reverse else -1
        for t in range(tiles):
            q, to = (p, t + step) if 0 <= t + step < tiles else (p ^ 1, t)
            route.append((p * tiles + t, q * tiles + to))
    return lax.ppermute(value, ("panel", "tile"), route)


def body(adjoint_new, weights, departure, send_point, block_count, rotation):
    fields, levels, cells = adjoint_new.shape
    blocks, slots = send_point.shape
    stencil = departure.shape[0]
    rows = fields * levels
    count = lax.axis_size("lev")
    paired = lax.axis_size("panel") % 2 == 0
    points = blocks * slots
    early = 1
    shape = jax.ShapeDtypeStruct
    parts = [rotated(weights, "lev", s) for s in range(1, count)]
    inputs = (
        adjoint_new.reshape(rows, cells), weights, departure, send_point,
        block_count.reshape(1, -1), rotation.reshape(1, -1),
    )
    sums = shape((cells // LO * 2 * rows, LO), F32)
    u, own, dep, keep, picked, *slot_rows, acc = pl.pallas_call(
        lambda *refs: prepare_kernel(levels, early, *refs),
        out_shape=[
            shape((rows, cells), F32),
            shape(weights.shape, F32),
            shape((stencil, cells), I32),
            shape((stencil, cells), F32),
            shape((rows + SUB, points), F32),
            *([shape((blocks, slots), I32)] * 3),
            sums,
        ],
        in_specs=[HBM] * 6,
        out_specs=[VMEM] * 9,
        scratch_shapes=[
            pltpu.VMEM((blocks, slots), I32),
            pltpu.VMEM((1, block_count.size), I32),
            pltpu.VMEM((1, rotation.size), I32),
            pltpu.SemaphoreType.DMA((6,)),
        ],
        cost_estimate=pl.CostEstimate(
            flops=4 * rows * cells * points, bytes_accessed=8 * rows * cells, transcendentals=0
        ),
        compiler_params=PARAMS,
        name="prepare",
    )(*(pltpu.with_memory_space_constraint(a, pltpu.HBM) for a in inputs))
    block = shape((rows + SUB, slots), F32)
    *outgoing, full = pl.pallas_call(
        lambda *refs: send_kernel(count, paired, *refs),
        out_shape=[block] * blocks + [shape((stencil, cells), F32)],
        in_specs=[VMEM] * (4 + count),
        out_specs=[VMEM] * (blocks + 1),
        compiler_params=PARAMS,
        name="send",
    )(picked, *slot_rows, own, *parts)
    if paired:
        back, forth = (lambda v: racetrack(v, True)), (lambda v: racetrack(v, False))
    else:
        back, forth = (lambda v: rotated(v, "tile", -1)), (lambda v: rotated(v, "tile", 1))
    received = [
        back(outgoing[0]),
        rotated(outgoing[1], "panel", 1),
        forth(outgoing[2]),
        rotated(outgoing[3], "panel", -1),
    ]
    acc = pl.pallas_call(
        lambda *refs: local_kernel(early, count, *refs),
        out_shape=sums,
        in_specs=[VMEM] * 5,
        out_specs=VMEM,
        cost_estimate=pl.CostEstimate(
            flops=4 * rows * cells * stencil * cells, bytes_accessed=8 * rows * cells, transcendentals=0
        ),
        compiler_params=PARAMS,
        name="local",
    )(u, dep, full, keep, acc)
    result = shape((rows, cells), F32)
    merged = pl.pallas_call(
        merge_kernel,
        out_shape=result,
        in_specs=[VMEM] * (blocks - 1),
        out_specs=VMEM,
        cost_estimate=pl.CostEstimate(
            flops=4 * rows * cells * points, bytes_accessed=8 * rows * cells, transcendentals=0
        ),
        compiler_params=PARAMS,
        name="merge",
    )(acc, *received[:-2])
    out = pl.pallas_call(
        arrive_kernel,
        out_shape=result,
        in_specs=[VMEM] * 3,
        out_specs=VMEM,
        compiler_params=PARAMS,
        name="arrive",
    )(merged, *received[-2:])
    return out.reshape(fields, levels, cells)


def solution(mesh):
    return jax.shard_map(
        body,
        mesh=mesh,
        in_specs=(
            P(None, "lev", ("panel", "tile")),
            P(None, ("panel", "tile", "lev")),
            P(None, ("panel", "tile")),
            P(None, ("panel", "tile")),
            P(None, ("panel", "tile")),
            P(None, ("panel", "tile")),
        ),
        out_specs=P(None, "lev", ("panel", "tile")),
        check_vma=False,
    )
```
